32 devices in a mesh: section: 2 (over x), azim: 4 (over z), axial: 4 (over y, core).
Axes of the slice: x: 2, y: 2, z: 4, core: 2. Of those that a mesh axis runs over, the one named last changes fastest.
Arguments:
- magnetic_vector_field: float32 [3, 4, 512, 512], P(None, 'azim', 'section', 'axial'), may hold values from -3 to 3
- imposed_current_density: float32 [3, 4, 512, 512], P(None, 'azim', 'section', 'axial'), may hold values from -6 to 6
- fixed_material_map: int32 [4, 512, 512], P('azim', 'section', 'axial'), may hold values from 0 to 7
- spinning_material_map: int32 [4, 128], replicated, may hold values from 0 to 7
- slab_slide_offsets: int32 [512], P('axial'), may hold values from 0 to 3, as said below
- inverse_permeability: float32 [8], replicated, may hold values from 0.1 to 1
- electric_conductance: float32 [8], replicated, may hold values from 0.05 to 0.5
- core_dissipation_coefficient: float32 [8], replicated, may hold values from 0.2 to 2
- inplane_thermal_conductance: float32 [8], replicated, may hold values from 1 to 4
- through_plane_conductance: float32 [8], replicated, may hold values from 0.1 to 0.5
- thermal_storage: float32 [8], replicated, may hold values from 0.05 to 0.3
- prior_thermal_state: float32 [4, 512, 512], P(None, ('section', 'azim'), 'axial'), may hold values from -6 to 6
- goal_sensitivity: float32 [4, 512, 512], P(None, ('section', 'azim'), 'axial'), may hold values from -16 to 16
Outputs:
- magnetic_misfit: float32 [3, 4, 512, 512], P(None, 'azim', 'section', 'axial')
- dual_magnetic_rhs: float32 [3, 4, 512, 512], P(None, 'azim', 'section', 'axial')
- thermal_state: float32 [4, 512, 512], P('azim', 'section', 'axial')
The draws below stay inside these ranges and needn't reach their ends.
Inputs may be any that keep to these rules, and one draw needn't show every extreme that they name: `slab_slide_offsets`: the smallest and the largest offset each occur at some layer.
All inputs are finite; a program needn't handle non-finite values.
Results may differ from the reference program's by a relative error of at most 0.00002.
Values sent between devices are 32-bit elements; how exact they have to be, the bound alone decides.
A program may use at most 64 MiB of HBM per device.

```python
import math
import jax
import jax.numpy as jnp

NREG = 8
SWEEPS = 4
ANGULAR_BINS = 4
RADIUS_BINS = 512
LENGTHWISE_SLABS = 512
RROT = 128


def draw_slab_slide_offsets(key, part):
    first, second = jax.random.split(jax.random.fold_in(key, 11))
    offsets = jax.random.randint(first, (LENGTHWISE_SLABS,), 0, ANGULAR_BINS)
    places = jax.random.permutation(second, LENGTHWISE_SLABS)
    offsets = offsets.at[places[0]].set(0)
    offsets = offsets.at[places[1]].set(ANGULAR_BINS - 1)
    return offsets.astype(jnp.int32)


def draw_goal_sensitivity(key, part):
    shape = (ANGULAR_BINS, RADIUS_BINS, LENGTHWISE_SLABS)
    return jnp.clip(4.0 * jax.random.normal(key, shape, jnp.float32), -16.0, 16.0)


def set_ends(drawn, own_key, low, largest):
    place = [jax.random.randint(jax.random.fold_in(own_key, axis), (), 0, length) for axis, length in enumerate(drawn.shape)]
    main_axis = drawn.shape.index(max(drawn.shape))
    beside = place[:main_axis] + [(place[main_axis] + 1) % drawn.shape[main_axis]] + place[main_axis + 1:]
    return drawn.at[tuple(place)].set(low).at[tuple(beside)].set(largest)


def block_scale(own_key, extent, cuts, least, high):
    def one(axis_at, blocks):
        steps = jax.random.uniform(jax.random.fold_in(jax.random.fold_in(own_key, 6), axis_at), (blocks,), jnp.float32, least / len(cuts), high / len(cuts))
        return jnp.repeat(jnp.exp(steps), extent[axis_at] // blocks).reshape((-1,) + (1,) * (len(extent) - axis_at - 1))

    level = one(*cuts[0])
    for cut in cuts[1:]:
        level = level * one(*cut)
    return level


def centred(key, dims, width, limit, cuts=(), kind=jnp.bfloat16):
    level = block_scale(key, dims, cuts, -0.22, 0.18) if cuts else 1.0
    values = jax.random.normal(key, dims, jnp.float32) * width * level
    return jnp.minimum(jnp.maximum(values, -limit), limit).astype(kind)


def setup_inputs(seed: int = 0) -> dict:
    key_list = jax.random.split(jax.random.key(seed), 14)
    magnetic_vector_field = centred(key_list[0], (3, ANGULAR_BINS, RADIUS_BINS, LENGTHWISE_SLABS), 0.5, 3.0, ((1, 4), (2, 2), (3, 4)), jnp.float32)
    imposed_current_density = centred(key_list[1], (3, ANGULAR_BINS, RADIUS_BINS, LENGTHWISE_SLABS), 1.0, 6.0, ((1, 4), (2, 2), (3, 4)), jnp.float32)
    fixed_material_map = set_ends(jax.random.randint(key_list[2], (ANGULAR_BINS, RADIUS_BINS, LENGTHWISE_SLABS), 0, NREG), jax.random.fold_in(key_list[2], 1), 0, NREG - 1).astype(jnp.int32)
    spinning_material_map = set_ends(jax.random.randint(key_list[3], (ANGULAR_BINS, RROT), 0, NREG), jax.random.fold_in(key_list[3], 1), 0, NREG - 1).astype(jnp.int32)
    slab_slide_offsets = draw_slab_slide_offsets(jax.random.fold_in(key_list[13], 71), 0)
    inverse_permeability = jnp.clip(jnp.exp(jax.random.uniform(key_list[5], (NREG,), jnp.float32, math.log(0.1), math.log(1.0))), 0.1, 1.0)
    electric_conductance = jnp.clip(jnp.exp(jax.random.uniform(key_list[6], (NREG,), jnp.float32, math.log(0.05), math.log(0.5))), 0.05, 0.5)
    core_dissipation_coefficient = jnp.clip(jnp.exp(jax.random.uniform(key_list[7], (NREG,), jnp.float32, math.log(0.2), math.log(2.0))), 0.2, 2.0)
    inplane_thermal_conductance = jnp.clip(jnp.exp(jax.random.uniform(key_list[8], (NREG,), jnp.float32, math.log(1.0), math.log(4.0))), 1.0, 4.0)
    through_plane_conductance = jnp.clip(jnp.exp(jax.random.uniform(key_list[9], (NREG,), jnp.float32, math.log(0.1), math.log(0.5))), 0.1, 0.5)
    thermal_storage = jnp.clip(jnp.exp(jax.random.uniform(key_list[10], (NREG,), jnp.float32, math.log(0.05), math.log(0.3))), 0.05, 0.3)
    prior_thermal_state = centred(key_list[11], (ANGULAR_BINS, RADIUS_BINS, LENGTHWISE_SLABS), 1.0, 6.0, ((1, 8), (2, 4)), jnp.float32)
    goal_sensitivity = draw_goal_sensitivity(jax.random.fold_in(key_list[13], 71), 0)
    return {"magnetic_vector_field": magnetic_vector_field, "imposed_current_density": imposed_current_density, "fixed_material_map": fixed_material_map, "spinning_material_map": spinning_material_map, "slab_slide_offsets": slab_slide_offsets, "inverse_permeability": inverse_permeability, "electric_conductance": electric_conductance, "core_dissipation_coefficient": core_dissipation_coefficient, "inplane_thermal_conductance": inplane_thermal_conductance, "through_plane_conductance": through_plane_conductance, "thermal_storage": thermal_storage, "prior_thermal_state": prior_thermal_state, "goal_sensitivity": goal_sensitivity}


def region_map(fixed_material_map, spinning_material_map, slab_slide_offsets, azim_cells, radial_cells, azim_total):
    shifted = jnp.mod(azim_cells[:, None] - slab_slide_offsets[None, :], azim_total).astype(jnp.int32)
    rotor_rows = jnp.transpose(spinning_material_map[shifted], (0, 2, 1))
    extra = fixed_material_map.shape[1] - rotor_rows.shape[1]
    rotor_rows = jnp.pad(rotor_rows, ((0, 0), (0, extra), (0, 0)))
    inside = (radial_cells < spinning_material_map.shape[1])[None, :, None]
    return jnp.where(inside, rotor_rows, fixed_material_map)


def lookup(regions, materials):
    results = [jnp.zeros(regions.shape, jnp.float32) for material in materials]
    for region in range(NREG):
        matches = regions == region
        results = [jnp.where(matches, material[region], result) for material, result in zip(materials, results)]
    return results


def forward_diff(values, axis_dim):
    difference = jnp.diff(values, axis=axis_dim)
    window = [slice(0, -1), slice(0, -1), slice(0, -1)]
    window[axis_dim] = slice(None)
    return difference[tuple(window)]


def backward_diff(values, axis_dim):
    difference = -jnp.diff(values, axis=axis_dim)
    window = [slice(1, None), slice(1, None), slice(1, None)]
    window[axis_dim] = slice(None)
    return difference[tuple(window)]


def em_terms(padded):
    azim_part, radial_part, axial_part, reluct_pad = padded[0], padded[1], padded[2], padded[3]
    flux_azim = forward_diff(axial_part, 1) - forward_diff(radial_part, 2)
    flux_radial = forward_diff(azim_part, 2) - forward_diff(axial_part, 0)
    flux_axial = forward_diff(radial_part, 0) - forward_diff(azim_part, 1)
    reluct_cell = reluct_pad[:-1, :-1, :-1]
    field_azim = reluct_cell * flux_azim
    field_radial = reluct_cell * flux_radial
    field_axial = reluct_cell * flux_axial
    curl_azim = backward_diff(field_radial, 2) - backward_diff(field_axial, 1)
    curl_radial = backward_diff(field_axial, 0) - backward_diff(field_azim, 2)
    curl_axial = backward_diff(field_azim, 1) - backward_diff(field_radial, 0)
    curl_term = jnp.stack([curl_azim, curl_radial, curl_axial])
    flux = jnp.stack([flux_azim, flux_radial, flux_axial])[:, 1:, 1:, 1:]
    return curl_term, flux


def relax(padded, local_thermal_storage, right_hand_sides):
    interior = padded[:, :, 1:-1, 1:-1]
    repeat_relaxation_passes = interior[:2]
    plane_cell = interior[2]
    axial_cell = interior[3]
    faces = [
        (jnp.roll(repeat_relaxation_passes, -1, axis=1), jnp.roll(plane_cell, -1, axis=0), plane_cell),
        (jnp.roll(repeat_relaxation_passes, 1, axis=1), jnp.roll(plane_cell, 1, axis=0), plane_cell),
        (padded[:2, :, 2:, 1:-1], padded[2, :, 2:, 1:-1], plane_cell),
        (padded[:2, :, :-2, 1:-1], padded[2, :, :-2, 1:-1], plane_cell),
        (padded[:2, :, 1:-1, 2:], padded[3, :, 1:-1, 2:], axial_cell),
        (padded[:2, :, 1:-1, :-2], padded[3, :, 1:-1, :-2], axial_cell),
    ]
    weight_sum = jnp.zeros(plane_cell.shape, jnp.float32)
    inflow = jnp.zeros(repeat_relaxation_passes.shape, jnp.float32)
    for neighbour, beside, own in faces:
        weight = 0.5 * (own + beside)
        weight_sum = weight_sum + weight
        inflow = inflow + weight * neighbour
    return (right_hand_sides + inflow) / (local_thermal_storage + weight_sum)


def pad_grid(stacked):
    wrapped = jnp.concatenate([stacked[:, -1:], stacked, stacked[:, :1]], axis=1)
    return jnp.pad(wrapped, ((0, 0), (0, 0), (1, 1), (1, 1)))


def reference(magnetic_vector_field, imposed_current_density, fixed_material_map, spinning_material_map, slab_slide_offsets, inverse_permeability, electric_conductance, core_dissipation_coefficient, inplane_thermal_conductance, through_plane_conductance, thermal_storage, prior_thermal_state, goal_sensitivity):
    azim_cells = jnp.arange(ANGULAR_BINS, dtype=jnp.int32)
    radial_cells = jnp.arange(RADIUS_BINS, dtype=jnp.int32)
    regions = region_map(fixed_material_map, spinning_material_map, slab_slide_offsets, azim_cells, radial_cells, ANGULAR_BINS)
    reluct_cell, eddy_cell, loss_cell = lookup(regions, (inverse_permeability, electric_conductance, core_dissipation_coefficient))
    plane_cell, axial_cell, local_thermal_storage = lookup(regions, (inplane_thermal_conductance, through_plane_conductance, thermal_storage))
    stacked = jnp.concatenate([magnetic_vector_field, reluct_cell[None]], axis=0)
    curl_term, flux = em_terms(pad_grid(stacked))
    magnetic_misfit = curl_term + eddy_cell * magnetic_vector_field - imposed_current_density
    thermal_rhs = loss_cell * jnp.sum(flux * flux, axis=0)
    right_hand_sides = jnp.stack([local_thermal_storage * prior_thermal_state + thermal_rhs, goal_sensitivity])
    repeat_relaxation_passes = jnp.stack([prior_thermal_state, jnp.zeros_like(prior_thermal_state)])
    for iteration in range(SWEEPS):
        combined = jnp.concatenate([repeat_relaxation_passes, plane_cell[None], axial_cell[None]], axis=0)
        padded = jnp.pad(combined, ((0, 0), (0, 0), (1, 1), (1, 1)))
        repeat_relaxation_passes = relax(padded, local_thermal_storage, right_hand_sides)
    thermal_state = repeat_relaxation_passes[0]
    dual_magnetic_rhs = 2.0 * loss_cell * repeat_relaxation_passes[1] * flux
    return magnetic_misfit, dual_magnetic_rhs, thermal_state
```

```python
import functools

import jax
import jax.numpy as jnp
from jax import lax
from jax.experimental import pallas as pl
from jax.experimental.pallas import tpu as pltpu
from jax.sharding import PartitionSpec as P

SWEEPS = 4
RIM = 8
MESH = pl.DeviceIdType.MESH


def pick(bits, table):
    low, mid, high = bits
    pairs = [jnp.where(low, table[2 * i + 1], table[2 * i]) for i in range(4)]
    return jnp.where(high, jnp.where(mid, pairs[3], pairs[2]), jnp.where(mid, pairs[1], pairs[0]))


def bits_of(regions):
    return ((regions & 1) != 0, (regions & 2) != 0, (regions & 4) != 0)


def kernel(sizes, *refs):
    S, N, C = sizes
    (A_hbm, J_hbm, fixed, spin, offs, t_rel, t_eddy, t_loss, t_plane, t_axial, t_cap, prior, goal,
     misfit, dual, temp,
     AN, AX, AR, HN, HX, HR, regE, lossM, srcE, flux, H,
     priorX, goalX, regX, srcX,
     wa, wr, wl, inv, capH, rhsT, vT, vA, finT, finA, retA,
     A, J, relayG, relayP, local, send, recv) = refs
    R, L = fixed.shape
    rows = prior.shape[1]
    RROT = spin.shape[1]
    ext = rows + 2 * RIM
    s, j, c = lax.axis_index("section"), lax.axis_index("azim"), lax.axis_index("axial")
    Q = S * N
    q = s * N + j

    def section_id(d):
        return (lax.rem(s + d + S, S), j, c)

    def axial_id(d):
        return (s, j, lax.rem(c + d + C, C))

    def azim_id(d):
        return (s, lax.rem(j + d + N, N), c)

    barrier = pltpu.get_barrier_semaphore()
    partners = [azim_id(d) for d in range(1, N)]
    partners += [near(d) for near in (section_id, axial_id) for d in (1, -1)]
    for partner in partners:
        pl.semaphore_signal(barrier, inc=1, device_id=partner, device_id_type=MESH)

    loads = [
        pltpu.make_async_copy(A_hbm, A, local.at[0]),
        pltpu.make_async_copy(goal, goalX.at[1, :, pl.ds(RIM, rows), :], local.at[1]),
        pltpu.make_async_copy(prior, priorX.at[1, :, pl.ds(RIM, rows), :], local.at[2]),
        pltpu.make_async_copy(J_hbm, J, local.at[3]),
    ]
    for load in loads:
        load.start()

    counter = [0]
    pending = []
    finals = []

    def slots(count):
        k = counter[0]
        counter[0] += count
        return k

    def remote(src, dst, device, k):
        return pltpu.make_async_remote_copy(
            src_ref=src, dst_ref=dst, send_sem=send.at[k], recv_sem=recv.at[k],
            device_id=device, device_id_type=MESH)

    def when(cond, f):
        if cond is None:
            f()
        else:
            pl.when(cond)(f)

    def copy(src, dst, device, sending=None, receiving=None):
        desc = remote(src, dst, device, slots(1))
        when(sending, lambda: desc.start())
        pending.append((desc, sending))
        return lambda: when(receiving, lambda: desc.wait_recv())

    def farthest(i):
        return jnp.where(j < N // 2, N - i, i)

    def both(*conds):
        return functools.reduce(jnp.logical_and, conds)

    top, bottom = j == 0, j == N - 1
    before, after = s > 0, s < S - 1

    def forward(X):
        return [copy(X.at[1], X.at[2], axial_id(-1), c > 0, c < C - 1),
                copy(X.at[1], X.at[0], axial_id(1), c < C - 1, c > 0)]

    def centre(src, X):
        part = pl.ds(RIM, rows)
        return [copy(src, X.at[2, :, part, :], axial_id(-1), c > 0, c < C - 1),
                copy(src, X.at[0, :, part, :], axial_id(1), c < C - 1, c > 0)]

    def outer(X):
        arrivals = []
        for part in (pl.ds(0, RIM), pl.ds(RIM + rows, RIM)):
            own = X.at[1, :, part, :]
            arrivals.append(copy(own, X.at[2, :, part, :], axial_id(-1), c > 0, c < C - 1))
            arrivals.append(copy(own, X.at[0, :, part, :], axial_id(1), c < C - 1, c > 0))
        return arrivals

    def rims(src, X, relay):
        low, high = X.at[1, :, pl.ds(0, RIM), :], X.at[1, :, pl.ds(RIM + rows, RIM), :]
        first, last = src.at[:, 0:RIM, :], src.at[:, rows - RIM:rows, :]
        arrivals = [
            copy(last, low, azim_id(1), jnp.logical_not(bottom), jnp.logical_not(top)),
            copy(first, high, azim_id(-1), jnp.logical_not(top), jnp.logical_not(bottom))]
        crossed = [
            copy(last, relay.at[0], section_id(1), both(bottom, after), both(bottom, before)),
            copy(first, relay.at[1], section_id(-1), both(top, before), both(top, after))]

        def relayed():
            for arrive in crossed:
                arrive()
            arrivals.append(copy(relay.at[0], low, azim_id(1), both(bottom, before), both(top, before)))
            arrivals.append(copy(relay.at[1], high, azim_id(-1), both(top, after), both(bottom, after)))
            return arrivals
        return relayed

    def spread(E, target):
        inner = ext - RIM

        def block(peer, slot, low, high, owner=j):
            first, count = (RIM if low else 0), (inner if low or high else ext)
            return remote(
                E.at[pl.ds(pl.multiple_of(peer * rows + first, 8), count), :],
                target.at[1, owner, pl.ds(first, count), :], (s, peer, c), slot)

        def cases(peer, f):
            pl.when(peer == 0)(lambda: f(True, False))
            pl.when(peer == N - 1)(lambda: f(False, True))
            pl.when(both(peer > 0, peer < N - 1))(lambda: f(False, False))

        k = slots(N - 1)
        for i in range(1, N):
            d = farthest(i)
            peer = lax.rem(j + d, N)
            cases(peer, lambda low, high: block(peer, k + d - 1, low, high).start())
        for d in range(1, N):
            peer = lax.rem(j + d, N)
            finals.append(lambda peer=peer, d=d: cases(
                peer, lambda low, high: block(peer, k + d - 1, low, high).wait_send()))
        edges = [copy(E.at[R:R + RIM, :], E.at[0:RIM, :], section_id(1), after, before),
                 copy(E.at[RIM:2 * RIM, :], E.at[R + RIM:R + 2 * RIM, :], section_id(-1), before, after)]

        def rest():
            for arrive in edges:
                arrive()
            ends = []
            for peer, start, there in ((0, 0, before), (N - 1, RIM + rows, after)):
                b = slots(N - 1)
                d = lax.rem(peer - j + N, N)
                own = E.at[start if peer == 0 else R + RIM:(start if peer == 0 else R + RIM) + RIM, :]
                away = both(there, j != peer)
                desc = remote(own, target.at[1, j, pl.ds(start, RIM), :], (s, peer, c),
                              b + jnp.where(d > 0, d - 1, 0))
                pl.when(away)(lambda desc=desc: desc.start())
                pending.append((desc, away))
                for d in range(1, N):
                    got = remote(own, target.at[1, lax.rem(j - d + N, N), pl.ds(start, RIM), :],
                                 (s, peer, c), b + d - 1)
                    ends.append((got, both(there, j == peer)))
            target[1, j] = E[pl.ds(pl.multiple_of(j * rows, 8), ext), :]

            def arrived():
                for d in range(1, N):
                    owner = lax.rem(j - d + N, N)
                    cases(j, lambda low, high: block(j, k + d - 1, low, high, owner).wait_recv())
                for got, here in ends:
                    pl.when(here)(lambda got=got: got.wait_recv())
            return arrived
        return rest

    pl.semaphore_wait(barrier, len(partners))

    got_an = copy(A_hbm.at[1:3], AN, azim_id(-1))
    got_ax = copy(A_hbm.at[0:2], AX, axial_id(-1), c > 0, c < C - 1)
    got_ar = copy(A_hbm.at[:, 0:RIM, :], AR, section_id(-1), before, after)

    lane = lax.broadcasted_iota(jnp.int32, (R, L), 1)
    row = lax.broadcasted_iota(jnp.int32, (R, L), 0)
    shift = j - offs[...]
    shift = jnp.broadcast_to(jnp.where(shift < 0, shift + N, shift), (RROT, L))
    rotor = jnp.zeros((RROT, L), jnp.float32)
    for m in range(N):
        column = jnp.transpose(jnp.broadcast_to(spin[m:m + 1, :].astype(jnp.float32), (L, RROT)))
        rotor = jnp.where(shift == m, column, rotor)
    regE[RIM:RIM + R, :] = fixed[...]
    regE[RIM:RIM + RROT, :] = jnp.where(s == 0, rotor.astype(jnp.int32), fixed[0:RROT, :])

    rest_reg = spread(regE, regX)
    rest_goal = rims(goal, goalX, relayG)
    rest_prior = rims(prior, priorX, relayP)
    goal_centre, prior_centre = centre(goal, goalX), centre(prior, priorX)
    lossM[...] = pick(bits_of(regE[RIM:RIM + R, :]), t_loss)
    got_reg = rest_reg()
    got_goal, got_prior = rest_goal(), rest_prior()

    loads[0].wait()

    got_ax()
    got_ar()
    last_lane, last_row = c == C - 1, s == S - 1

    def lane_up(values, beside):
        beside = jnp.where(last_lane, 0.0, beside)
        return pltpu.roll(jnp.where(lane == 0, beside, values), L - 1, 1)

    def row_up(values, beside):
        beside = jnp.where(last_row, 0.0, beside)
        return jnp.where(row == R - 1, beside, pltpu.roll(values, R - 1, 0))

    flux[0] = (row_up(A[2], AR[2, 0:1, :]) - A[2]) - (lane_up(A[1], AX[1]) - A[1])
    flux[1] = lane_up(A[0], AX[0]) - A[0]
    flux[2] = A[0] - row_up(A[0], AR[0, 0:1, :])
    got_an()
    f0 = flux[0]
    f1 = flux[1] - (AN[1] - A[2])
    f2 = flux[2] + (AN[0] - A[1])
    flux[1] = f1
    flux[2] = f2
    srcE[RIM:RIM + R, :] = lossM[...] * (f0 * f0 + f1 * f1 + f2 * f2)
    rest_src = spread(srcE, srcX)
    reluct = pick(bits_of(regE[RIM:RIM + R, :]), t_rel)
    H[0] = reluct * flux[0]
    H[1] = reluct * flux[1]
    H[2] = reluct * flux[2]
    got_hr = copy(H.at[:, R - RIM:R, :], HR, section_id(1), after, before)
    got_src = rest_src()

    got_reg()
    got_reg = forward(regX)
    for load, arrivals in ((loads[1], got_goal), (loads[2], got_prior)):
        load.wait()
        for arrive in arrivals:
            arrive()
    got_goal = goal_centre + outer(goalX)
    got_prior = prior_centre + outer(priorX)

    got_src()
    got_src = forward(srcX)
    ring = remote(H.at[1:3], HN, azim_id(1), slots(1))
    pl.when(j < N - 1)(lambda: ring.start())
    got_hx = copy(H.at[0:2], HX, axial_id(1), c < C - 1, c > 0)

    def ext_mask():
        grow = lax.broadcasted_iota(jnp.int32, (ext, 2 * L), 0) + (q * rows - RIM)
        glane = lax.broadcasted_iota(jnp.int32, (ext, 2 * L), 1)
        ok = jnp.logical_and(grow >= 0, grow < Q * rows)
        right = jnp.logical_and(glane >= L, glane < L + L // 2)
        left = glane >= L + L // 2
        ok = jnp.logical_and(ok, jnp.logical_not(jnp.logical_and(right, c == C - 1)))
        return jnp.logical_and(ok, jnp.logical_not(jnp.logical_and(left, c == 0)))

    half = lax.broadcasted_iota(jnp.int32, (ext, L), 1) < L // 2

    def wide(X, a):
        return jnp.concatenate([X[1, a], jnp.where(half, X[2, a], X[0, a])], axis=1)

    up = lambda x, axis: pltpu.roll(x, x.shape[axis] - 1, axis)
    down = lambda x, axis: pltpu.roll(x, 1, axis)

    def each(f):
        if N <= 8:
            for a in range(N):
                f(a, (a + 1) % N, (a + N - 1) % N)
        else:
            def step(a, carry):
                f(a, lax.rem(a + 1, N), lax.rem(a + N - 1, N))
                return carry
            lax.fori_loop(0, N, step, 0)

    for arrive in got_reg:
        arrive()

    def first(a, ap, am):
        bits = bits_of(wide(regX, a))
        ok = ext_mask()
        plane = jnp.where(ok, pick(bits, t_plane), 0.0)
        axial = jnp.where(ok, pick(bits, t_axial), 0.0)
        capH[a] = pick(bits, t_cap)
        inv[a] = plane
        wr[a] = 0.5 * (plane + up(plane, 0))
        wl[a] = 0.5 * (axial + up(axial, 1))

    def second(a, ap, am):
        wa[a] = 0.5 * (inv[a] + inv[ap])

    def third(a, ap, am):
        total = (wa[a] + wa[am]) + (wr[a] + down(wr[a], 0)) + (wl[a] + down(wl[a], 1)) + capH[a]
        inv[a] = jnp.where(ext_mask(), 1.0 / total, 0.0)

    each(first)
    each(second)
    each(third)

    def inflow(v, a, ap, am):
        x = v[a]
        r, l = wr[a], wl[a]
        return ((wa[a] * v[ap] + wa[am] * v[am]) + (r * up(x, 0) + down(r * x, 0))
                + (l * up(x, 1) + down(l * x, 1)))

    for arrive in got_goal:
        arrive()

    def adjoint_first(a, ap, am):
        rhs = jnp.where(ext_mask(), wide(goalX, a), 0.0)
        rhsT[a] = rhs
        vA[0, a] = rhs * inv[a]

    each(adjoint_first)

    def sweeps(v, count, final):
        for k in range(count):
            now, later = k % 2, (k + 1) % 2

            def one(a, ap, am):
                new = (rhsT[a] + inflow(v.at[now], a, ap, am)) * inv[a]
                if k == count - 1:
                    final[a] = new[RIM:RIM + rows, 0:L]
                else:
                    v[later, a] = new
            each(one)

    def gather(final, ret):
        k = slots(N - 1)

        def part(peer, slot, owner=j):
            return remote(final.at[peer], ret.at[pl.ds(pl.multiple_of(owner * rows, 8), rows), :],
                          (s, peer, c), slot)

        for i in range(1, N):
            d = farthest(i)
            peer = lax.rem(j + d, N)
            part(peer, k + d - 1).start()
        ret[pl.ds(pl.multiple_of(j * rows, 8), rows), :] = final[j]
        arrivals = []
        for d in range(1, N):
            pending.append((part(lax.rem(j + d, N), k + d - 1), None))
            owner = lax.rem(j - d + N, N)
            arrivals.append(lambda d=d, owner=owner: part(j, k + d - 1, owner).wait_recv())
        return arrivals

    sweeps(vA, SWEEPS - 1, finA)
    got_adj = gather(finA, retA)
    pl.when(j == N - 1)(lambda: ring.start())
    pending.append((ring, None))

    for arrive in got_prior:
        arrive()
    for arrive in got_src:
        arrive()

    def thermal_first(a, ap, am):
        ok = ext_mask()
        start = jnp.where(ok, wide(priorX, a), 0.0)
        vT[0, a] = start
        rhsT[a] = capH[a] * start + jnp.where(ok, wide(srcX, a), 0.0)

    each(thermal_first)
    sweeps(vT, SWEEPS, finT)
    got_temp = gather(finT, temp)

    loads[3].wait()
    ring.wait_recv()
    got_hx()
    got_hr()

    def lane_down(values, beside):
        beside = jnp.where(c == 0, 0.0, beside)
        return pltpu.roll(jnp.where(lane == L - 1, beside, values), 1, 1)

    def row_down(values, beside):
        beside = jnp.where(s == 0, 0.0, beside)
        return jnp.where(row == 0, beside, pltpu.roll(values, 1, 0))

    eddy = pick(bits_of(regE[RIM:RIM + R, :]), t_eddy)
    h0, h1, h2 = H[0], H[1], H[2]
    rim0, rim2 = HR[0, RIM - 1:RIM, :], HR[2, RIM - 1:RIM, :]
    misfit[0] = (lane_down(h1, HX[1]) - h1) - (row_down(h2, rim2) - h2) + eddy * A[0] - J[0]
    misfit[1] = (HN[1] - h2) - (lane_down(h0, HX[0]) - h0) + eddy * A[1] - J[1]
    misfit[2] = (row_down(h0, rim0) - h0) - (HN[0] - h1) + eddy * A[2] - J[2]

    for arrive in got_adj:
        arrive()
    scale = 2.0 * lossM[...] * retA[...]
    for k in range(3):
        dual[k] = scale * flux[k]
    for arrive in got_temp:
        arrive()
    for desc, sending in pending:
        when(sending, lambda: desc.wait_send())
    for final in finals:
        final()


def store(*refs):
    sems = refs[6]
    copies = [pltpu.make_async_copy(refs[k], refs[3 + k], sems.at[k]) for k in range(3)]
    for one in copies:
        one.start()
    for one in copies:
        one.wait()


def body(sizes, *args):
    (A, J, fixed, spin, offs, rel, eddy, loss, plane, axial, cap, prior, goal) = args
    _, one, R, L = A.shape
    assert one == 1 and spin.shape[1] <= R
    S, N, C = sizes
    rows = prior.shape[1]
    ext = rows + 2 * RIM
    f32 = jnp.float32
    vmem = pl.BlockSpec(memory_space=pltpu.VMEM)
    hbm = pl.BlockSpec(memory_space=pl.ANY)
    smem = pl.BlockSpec(memory_space=pltpu.SMEM)
    V = lambda *shape, dtype=f32: pltpu.VMEM(shape, dtype)
    copies = 38 + 8 * (N - 1)
    wide = (N, ext, 2 * L)
    misfit, dual, temp = pl.pallas_call(
        functools.partial(kernel, sizes),
        out_shape=(V(3, R, L), V(3, R, L), V(R, L)),
        in_specs=[hbm] * 2 + [vmem] * 3 + [smem] * 6 + [hbm] * 2,
        out_specs=(vmem, vmem, vmem),
        scratch_shapes=[
            V(2, R, L), V(2, R, L), V(3, RIM, L), V(2, R, L), V(2, R, L), V(3, RIM, L),
            V(R + 2 * RIM, L, dtype=jnp.int32), V(R, L), V(R + 2 * RIM, L), V(3, R, L), V(3, R, L),
            V(3, N, ext, L), V(3, N, ext, L), V(3, N, ext, L, dtype=jnp.int32), V(3, N, ext, L),
            V(*wide), V(*wide), V(*wide), V(*wide), V(*wide), V(*wide), V(2, *wide), V(2, *wide),
            V(N, rows, L), V(N, rows, L), V(R, L), V(3, R, L), V(3, R, L),
            V(2, N, RIM, L), V(2, N, RIM, L), pltpu.SemaphoreType.DMA((4,)),
            pltpu.SemaphoreType.DMA((copies,)), pltpu.SemaphoreType.DMA((copies,)),
        ],
        compiler_params=pltpu.CompilerParams(collective_id=0, has_side_effects=True),
    )(A.reshape(3, R, L), J.reshape(3, R, L), fixed.reshape(R, L), spin, offs.reshape(1, L),
      rel, eddy, loss, plane, axial, cap, prior, goal)
    misfit, dual, temp = pl.pallas_call(
        store,
        out_shape=tuple(jax.ShapeDtypeStruct(x.shape, f32) for x in (misfit, dual, temp)),
        in_specs=[vmem] * 3,
        out_specs=(hbm, hbm, hbm),
        scratch_shapes=[pltpu.SemaphoreType.DMA((3,))],
    )(*(pltpu.with_memory_space_constraint(x, pltpu.VMEM) for x in (misfit, dual, temp)))
    return misfit.reshape(3, 1, R, L), dual.reshape(3, 1, R, L), temp.reshape(1, R, L)


def solution(mesh):
    sizes = (mesh.shape["section"], mesh.shape["azim"], mesh.shape["axial"])
    in_specs = (
        P(None, "azim", "section", "axial"),
        P(None, "azim", "section", "axial"),
        P("azim", "section", "axial"),
        P(),
        P("axial"),
        P(),
        P(),
        P(),
        P(),
        P(),
        P(),
        P(None, ("section", "azim"), "axial"),
        P(None, ("section", "azim"), "axial"),
    )
    out_specs = (
        P(None, "azim", "section", "axial"),
        P(None, "azim", "section", "axial"),
        P("azim", "section", "axial"),
    )
    return jax.shard_map(functools.partial(body, sizes), mesh=mesh, in_specs=in_specs,
                         out_specs=out_specs, check_vma=False)
```

```python
import functools

import jax
import jax.numpy as jnp
from jax import lax
from jax.experimental import pallas as pl
from jax.experimental.pallas import tpu as pltpu
from jax.sharding import PartitionSpec as P

SWEEPS = 4
RIM = 8
MESH = pl.DeviceIdType.MESH


def pick(bits, table):
    low, mid, high = bits
    pairs = [jnp.where(low, table[2 * i + 1], table[2 * i]) for i in range(4)]
    return jnp.where(high, jnp.where(mid, pairs[3], pairs[2]), jnp.where(mid, pairs[1], pairs[0]))


def bits_of(regions):
    return ((regions & 1) != 0, (regions & 2) != 0, (regions & 4) != 0)


def kernel(sizes, *refs):
    S, N, C = sizes
    (A_hbm, J_hbm, fixed_hbm, spin_hbm, offs_hbm, *tables_hbm, prior, goal,
     misfit, dual, temp,
     fixed, spin, offs, t_rel, t_eddy, t_loss, t_plane, t_axial, t_cap,
     AN, AX, AR, HN, HX, HR, regE, lossM, srcE, flux, H,
     priorX, goalX, regX, srcX, priorS, goalS, regS, srcS, priorP, goalP, regP, srcP,
     wa, wr, wl, inv, capH, rhsT, vT, vA, finT, finA, retA,
     A, J, relayG, relayP, local, send, recv) = refs
    R, L = fixed.shape
    rows = prior.shape[1]
    RROT = spin.shape[1]
    ext = rows + 2 * RIM
    s, j, c = lax.axis_index("section"), lax.axis_index("azim"), lax.axis_index("axial")
    Q = S * N
    q = s * N + j

    def section_id(d):
        return (lax.rem(s + d + S, S), j, c)

    def axial_id(d):
        return (s, j, lax.rem(c + d + C, C))

    def azim_id(d):
        return (s, lax.rem(j + d + N, N), c)

    barrier = pltpu.get_barrier_semaphore()
    partners = [azim_id(d) for d in range(1, N)]
    partners += [near(d) for near in (section_id, axial_id) for d in (1, -1)]
    for partner in partners:
        pl.semaphore_signal(barrier, inc=1, device_id=partner, device_id_type=MESH)

    loads = [
        pltpu.make_async_copy(A_hbm, A, local.at[0]),
        pltpu.make_async_copy(goal, goalX.at[:, pl.ds(RIM, rows), :], local.at[1]),
        pltpu.make_async_copy(prior, priorX.at[:, pl.ds(RIM, rows), :], local.at[2]),
        pltpu.make_async_copy(J_hbm, J, local.at[3]),
    ]
    tables = (t_rel, t_eddy, t_loss, t_plane, t_axial, t_cap)
    maps = [pltpu.make_async_copy(src, dst, local.at[4 + k]) for k, (src, dst) in enumerate(
        zip((fixed_hbm, spin_hbm, offs_hbm, *tables_hbm), (fixed, spin, offs, *tables)))]
    loads = maps + loads
    for load in loads:
        load.start()
    loads = loads[len(maps):]

    counter = [0]
    pending = []
    finals = []

    def slots(count):
        k = counter[0]
        counter[0] += count
        return k

    def remote(src, dst, device, k):
        return pltpu.make_async_remote_copy(
            src_ref=src, dst_ref=dst, send_sem=send.at[k], recv_sem=recv.at[k],
            device_id=device, device_id_type=MESH)

    def when(cond, f):
        if cond is None:
            f()
        else:
            pl.when(cond)(f)

    def copy(src, dst, device, sending=None, receiving=None):
        desc = remote(src, dst, device, slots(1))
        when(sending, lambda: desc.start())
        pending.append((desc, sending))
        return lambda: when(receiving, lambda: desc.wait_recv())

    def farthest(i):
        return jnp.where(j < N // 2, N - i, i)

    def both(*conds):
        return functools.reduce(jnp.logical_and, conds)

    top, bottom = j == 0, j == N - 1
    before, after = s > 0, s < S - 1

    up = lambda x, axis: pltpu.roll(x, x.shape[axis] - 1, axis)
    down = lambda x, axis: pltpu.roll(x, 1, axis)

    def each(f):
        if N <= 8:
            for a in range(N):
                f(a, (a + 1) % N, (a + N - 1) % N)
        else:
            def step(a, carry):
                f(a, lax.rem(a + 1, N), lax.rem(a + N - 1, N))
                return carry
            lax.fori_loop(0, N, step, 0)

    G = L // N
    assert G >= SWEEPS
    place = lax.broadcasted_iota(jnp.int32, (ext, L), 1) // G

    def forward(X, sides, packed):
        def add(a, ap, am):
            x = pltpu.roll(X[a], a * G, 1)
            first = isinstance(a, int) and a == 0
            packed[0] = x if first else jnp.where(place == a, x, packed[0])
            packed[1] = x if first else jnp.where(place == am, x, packed[1])
        each(add)
        return [copy(packed.at[0], sides.at[1], axial_id(-1), c > 0, c < C - 1),
                copy(packed.at[1], sides.at[0], axial_id(1), c < C - 1, c > 0)]

    def wide(X, sides, a):
        beside = jnp.where(place == a, sides[1], sides[0])
        return jnp.concatenate([X[a], pltpu.roll(beside, (L - a * G) % L, 1)], axis=1)

    def rims(src, X, relay):
        low, high = X.at[:, pl.ds(0, RIM), :], X.at[:, pl.ds(RIM + rows, RIM), :]
        first, last = src.at[:, 0:RIM, :], src.at[:, rows - RIM:rows, :]
        arrivals = [
            copy(last, low, azim_id(1), jnp.logical_not(bottom), jnp.logical_not(top)),
            copy(first, high, azim_id(-1), jnp.logical_not(top), jnp.logical_not(bottom))]
        crossed = [
            copy(last, relay.at[0], section_id(1), both(bottom, after), both(bottom, before)),
            copy(first, relay.at[1], section_id(-1), both(top, before), both(top, after))]

        def relayed():
            for arrive in crossed:
                arrive()
            arrivals.append(copy(relay.at[0], low, azim_id(1), both(bottom, before), both(top, before)))
            arrivals.append(copy(relay.at[1], high, azim_id(-1), both(top, after), both(bottom, after)))
            return arrivals
        return relayed

    def spread(E, target):
        inner = ext - RIM

        def block(peer, slot, low, high, owner=j):
            first, count = (RIM if low else 0), (inner if low or high else ext)
            return remote(
                E.at[pl.ds(pl.multiple_of(peer * rows + first, 8), count), :],
                target.at[owner, pl.ds(first, count), :], (s, peer, c), slot)

        def cases(peer, f):
            pl.when(peer == 0)(lambda: f(True, False))
            pl.when(peer == N - 1)(lambda: f(False, True))
            pl.when(both(peer > 0, peer < N - 1))(lambda: f(False, False))

        k = slots(N - 1)
        for i in range(1, N):
            d = farthest(i)
            peer = lax.rem(j + d, N)
            cases(peer, lambda low, high: block(peer, k + d - 1, low, high).start())
        for d in range(1, N):
            peer = lax.rem(j + d, N)
            finals.append(lambda peer=peer, d=d: cases(
                peer, lambda low, high: block(peer, k + d - 1, low, high).wait_send()))
        edges = [copy(E.at[R:R + RIM, :], E.at[0:RIM, :], section_id(1), after, before),
                 copy(E.at[RIM:2 * RIM, :], E.at[R + RIM:R + 2 * RIM, :], section_id(-1), before, after)]

        def rest():
            for arrive in edges:
                arrive()
            ends = []
            for peer, start, there in ((0, 0, before), (N - 1, RIM + rows, after)):
                b = slots(N - 1)
                d = lax.rem(peer - j + N, N)
                own = E.at[start if peer == 0 else R + RIM:(start if peer == 0 else R + RIM) + RIM, :]
                away = both(there, j != peer)
                desc = remote(own, target.at[j, pl.ds(start, RIM), :], (s, peer, c),
                              b + jnp.where(d > 0, d - 1, 0))
                pl.when(away)(lambda desc=desc: desc.start())
                pending.append((desc, away))
                for d in range(1, N):
                    got = remote(own, target.at[lax.rem(j - d + N, N), pl.ds(start, RIM), :],
                                 (s, peer, c), b + d - 1)
                    ends.append((got, both(there, j == peer)))
            target[j] = E[pl.ds(pl.multiple_of(j * rows, 8), ext), :]

            def arrived():
                for d in range(1, N):
                    owner = lax.rem(j - d + N, N)
                    cases(j, lambda low, high: block(j, k + d - 1, low, high, owner).wait_recv())
                for got, here in ends:
                    pl.when(here)(lambda got=got: got.wait_recv())
            return arrived
        return rest

    pl.semaphore_wait(barrier, len(partners))

    got_an = copy(A_hbm.at[1:3], AN, azim_id(-1))
    got_ax = copy(A_hbm.at[0:2], AX, axial_id(-1), c > 0, c < C - 1)
    got_ar = copy(A_hbm.at[:, 0:RIM, :], AR, section_id(-1), before, after)

    for load in maps:
        load.wait()

    lane = lax.broadcasted_iota(jnp.int32, (R, L), 1)
    row = lax.broadcasted_iota(jnp.int32, (R, L), 0)
    shift = j - offs[...]
    shift = jnp.broadcast_to(jnp.where(shift < 0, shift + N, shift), (RROT, L))
    rotor = jnp.zeros((RROT, L), jnp.float32)
    for m in range(N):
        column = jnp.transpose(jnp.broadcast_to(spin[m:m + 1, :].astype(jnp.float32), (L, RROT)))
        rotor = jnp.where(shift == m, column, rotor)
    regE[RIM:RIM + R, :] = fixed[...]
    regE[RIM:RIM + RROT, :] = jnp.where(s == 0, rotor.astype(jnp.int32), fixed[0:RROT, :])

    rest_reg = spread(regE, regX)
    rest_goal = rims(goal, goalX, relayG)
    rest_prior = rims(prior, priorX, relayP)
    lossM[...] = pick(bits_of(regE[RIM:RIM + R, :]), t_loss)
    got_reg = rest_reg()
    got_goal, got_prior = rest_goal(), rest_prior()

    loads[0].wait()

    got_ax()
    got_ar()
    last_lane, last_row = c == C - 1, s == S - 1

    def lane_up(values, beside):
        beside = jnp.where(last_lane, 0.0, beside)
        return pltpu.roll(jnp.where(lane == 0, beside, values), L - 1, 1)

    def row_up(values, beside):
        beside = jnp.where(last_row, 0.0, beside)
        return jnp.where(row == R - 1, beside, pltpu.roll(values, R - 1, 0))

    flux[0] = (row_up(A[2], AR[2, 0:1, :]) - A[2]) - (lane_up(A[1], AX[1]) - A[1])
    flux[1] = lane_up(A[0], AX[0]) - A[0]
    flux[2] = A[0] - row_up(A[0], AR[0, 0:1, :])
    got_an()
    f0 = flux[0]
    f1 = flux[1] - (AN[1] - A[2])
    f2 = flux[2] + (AN[0] - A[1])
    flux[1] = f1
    flux[2] = f2
    srcE[RIM:RIM + R, :] = lossM[...] * (f0 * f0 + f1 * f1 + f2 * f2)
    rest_src = spread(srcE, srcX)
    reluct = pick(bits_of(regE[RIM:RIM + R, :]), t_rel)
    H[0] = reluct * flux[0]
    H[1] = reluct * flux[1]
    H[2] = reluct * flux[2]
    got_hr = copy(H.at[:, R - RIM:R, :], HR, section_id(1), after, before)
    got_src = rest_src()
    ring = [remote(H.at[1 + i // 1], HN.at[i // 1], azim_id(1), slots(1)) for i in range(2)]
    pending.extend((piece, None) for piece in ring)

    got_reg()
    got_reg = forward(regX, regS, regP)
    for load, arrivals in ((loads[1], got_goal), (loads[2], got_prior)):
        load.wait()
        for arrive in arrivals:
            arrive()
    got_goal = forward(goalX, goalS, goalP)
    got_prior = forward(priorX, priorS, priorP)

    got_src()
    got_src = forward(srcX, srcS, srcP)
    ring[0].start()
    pl.when(j < N - 1)(lambda: ring[1].start())
    got_hx = copy(H.at[0:2], HX, axial_id(1), c < C - 1, c > 0)

    def ext_mask():
        grow = lax.broadcasted_iota(jnp.int32, (ext, 2 * L), 0) + (q * rows - RIM)
        glane = lax.broadcasted_iota(jnp.int32, (ext, 2 * L), 1)
        ok = jnp.logical_and(grow >= 0, grow < Q * rows)
        right = jnp.logical_and(glane >= L, glane < L + L // 2)
        left = glane >= L + L // 2
        ok = jnp.logical_and(ok, jnp.logical_not(jnp.logical_and(right, c == C - 1)))
        return jnp.logical_and(ok, jnp.logical_not(jnp.logical_and(left, c == 0)))

    for arrive in got_reg:
        arrive()

    def first(a, ap, am):
        bits = bits_of(wide(regX, regS, a))
        ok = ext_mask()
        plane = jnp.where(ok, pick(bits, t_plane), 0.0)
        axial = jnp.where(ok, pick(bits, t_axial), 0.0)
        capH[a] = pick(bits, t_cap)
        inv[a] = plane
        wr[a] = 0.5 * (plane + up(plane, 0))
        wl[a] = 0.5 * (axial + up(axial, 1))

    def second(a, ap, am):
        wa[a] = 0.5 * (inv[a] + inv[ap])

    def third(a, ap, am):
        total = (wa[a] + wa[am]) + (wr[a] + down(wr[a], 0)) + (wl[a] + down(wl[a], 1)) + capH[a]
        inv[a] = jnp.where(ext_mask(), 1.0 / total, 0.0)

    each(first)
    each(second)
    each(third)

    def inflow(v, a, ap, am):
        x = v[a]
        r, l = wr[a], wl[a]
        return ((wa[a] * v[ap] + wa[am] * v[am]) + (r * up(x, 0) + down(r * x, 0))
                + (l * up(x, 1) + down(l * x, 1)))

    for arrive in got_goal:
        arrive()

    def adjoint_first(a, ap, am):
        rhs = jnp.where(ext_mask(), wide(goalX, goalS, a), 0.0)
        rhsT[a] = rhs
        vA[0, a] = rhs * inv[a]

    each(adjoint_first)

    def sweeps(v, count, final):
        for k in range(count):
            now, later = k % 2, (k + 1) % 2

            def one(a, ap, am):
                new = (rhsT[a] + inflow(v.at[now], a, ap, am)) * inv[a]
                if k == count - 1:
                    final[a] = new[RIM:RIM + rows, 0:L]
                else:
                    v[later, a] = new
            each(one)

    def gather(final, ret):
        k = slots(N - 1)

        def part(peer, slot, owner=j):
            return remote(final.at[peer], ret.at[pl.ds(pl.multiple_of(owner * rows, 8), rows), :],
                          (s, peer, c), slot)

        for i in range(1, N):
            d = farthest(i)
            peer = lax.rem(j + d, N)
            part(peer, k + d - 1).start()
        ret[pl.ds(pl.multiple_of(j * rows, 8), rows), :] = final[j]
        arrivals = []
        for d in range(1, N):
            pending.append((part(lax.rem(j + d, N), k + d - 1), None))
            owner = lax.rem(j - d + N, N)
            arrivals.append(lambda d=d, owner=owner: part(j, k + d - 1, owner).wait_recv())
        return arrivals

    sweeps(vA, SWEEPS - 1, finA)
    got_adj = gather(finA, retA)
    pl.when(j == N - 1)(lambda: ring[1].start())

    for arrive in got_prior:
        arrive()
    for arrive in got_src:
        arrive()

    def thermal_first(a, ap, am):
        ok = ext_mask()
        start = jnp.where(ok, wide(priorX, priorS, a), 0.0)
        vT[0, a] = start
        rhsT[a] = capH[a] * start + jnp.where(ok, wide(srcX, srcS, a), 0.0)

    each(thermal_first)
    sweeps(vT, SWEEPS, finT)
    got_temp = gather(finT, temp)

    loads[3].wait()
    for piece in ring:
        piece.wait_recv()
    got_hx()
    got_hr()

    def lane_down(values, beside):
        beside = jnp.where(c == 0, 0.0, beside)
        return pltpu.roll(jnp.where(lane == L - 1, beside, values), 1, 1)

    def row_down(values, beside):
        beside = jnp.where(s == 0, 0.0, beside)
        return jnp.where(row == 0, beside, pltpu.roll(values, 1, 0))

    eddy = pick(bits_of(regE[RIM:RIM + R, :]), t_eddy)
    h0, h1, h2 = H[0], H[1], H[2]
    rim0, rim2 = HR[0, RIM - 1:RIM, :], HR[2, RIM - 1:RIM, :]
    misfit[0] = (lane_down(h1, HX[1]) - h1) - (row_down(h2, rim2) - h2) + eddy * A[0] - J[0]
    misfit[1] = (HN[1] - h2) - (lane_down(h0, HX[0]) - h0) + eddy * A[1] - J[1]
    misfit[2] = (row_down(h0, rim0) - h0) - (HN[0] - h1) + eddy * A[2] - J[2]

    for arrive in got_adj:
        arrive()
    scale = 2.0 * lossM[...] * retA[...]
    for k in range(3):
        dual[k] = scale * flux[k]
    for arrive in got_temp:
        arrive()
    for desc, sending in pending:
        when(sending, lambda: desc.wait_send())
    for final in finals:
        final()


def store(*refs):
    sems = refs[6]
    copies = [pltpu.make_async_copy(refs[k], refs[3 + k], sems.at[k]) for k in range(3)]
    for one in copies:
        one.start()
    for one in copies:
        one.wait()


def body(sizes, *args):
    (A, J, fixed, spin, offs, rel, eddy, loss, plane, axial, cap, prior, goal) = args
    _, one, R, L = A.shape
    assert one == 1 and spin.shape[1] <= R
    S, N, C = sizes
    rows = prior.shape[1]
    ext = rows + 2 * RIM
    f32 = jnp.float32
    vmem = pl.BlockSpec(memory_space=pltpu.VMEM)
    hbm = pl.BlockSpec(memory_space=pl.ANY)
    V = lambda *shape, dtype=f32: pltpu.VMEM(shape, dtype)
    copies = 48 + 8 * (N - 1)
    wide = (N, ext, 2 * L)
    misfit, dual, temp = pl.pallas_call(
        functools.partial(kernel, sizes),
        out_shape=(V(3, R, L), V(3, R, L), V(R, L)),
        in_specs=[hbm] * 13,
        out_specs=(vmem, vmem, vmem),
        scratch_shapes=[
            V(R, L, dtype=jnp.int32), V(*spin.shape, dtype=jnp.int32), V(1, L, dtype=jnp.int32),
            *[pltpu.SMEM(table.shape, f32) for table in (rel, eddy, loss, plane, axial, cap)],
            V(2, R, L), V(2, R, L), V(3, RIM, L), V(2, R, L), V(2, R, L), V(3, RIM, L),
            V(R + 2 * RIM, L, dtype=jnp.int32), V(R, L), V(R + 2 * RIM, L), V(3, R, L), V(3, R, L),
            V(N, ext, L), V(N, ext, L), V(N, ext, L, dtype=jnp.int32), V(N, ext, L),
            *[V(2, ext, L, dtype=kind) for kind in (f32, f32, jnp.int32, f32)] * 2,
            V(*wide), V(*wide), V(*wide), V(*wide), V(*wide), V(*wide), V(2, *wide), V(2, *wide),
            V(N, rows, L), V(N, rows, L), V(R, L), V(3, R, L), V(3, R, L),
            V(2, N, RIM, L), V(2, N, RIM, L), pltpu.SemaphoreType.DMA((13,)),
            pltpu.SemaphoreType.DMA((copies,)), pltpu.SemaphoreType.DMA((copies,)),
        ],
        compiler_params=pltpu.CompilerParams(collective_id=0, has_side_effects=True),
    )(A.reshape(3, R, L), J.reshape(3, R, L), fixed.reshape(R, L), spin, offs.reshape(1, L),
      rel, eddy, loss, plane, axial, cap, prior, goal)
    misfit, dual, temp = pl.pallas_call(
        store,
        out_shape=tuple(jax.ShapeDtypeStruct(x.shape, f32) for x in (misfit, dual, temp)),
        in_specs=[vmem] * 3,
        out_specs=(hbm, hbm, hbm),
        scratch_shapes=[pltpu.SemaphoreType.DMA((3,))],
    )(*(pltpu.with_memory_space_constraint(x, pltpu.VMEM) for x in (misfit, dual, temp)))
    return misfit.reshape(3, 1, R, L), dual.reshape(3, 1, R, L), temp.reshape(1, R, L)


def solution(mesh):
    sizes = (mesh.shape["section"], mesh.shape["azim"], mesh.shape["axial"])
    in_specs = (
        P(None, "azim", "section", "axial"),
        P(None, "azim", "section", "axial"),
        P("azim", "section", "axial"),
        P(),
        P("axial"),
        P(),
        P(),
        P(),
        P(),
        P(),
        P(),
        P(None, ("section", "azim"), "axial"),
        P(None, ("section", "azim"), "axial"),
    )
    out_specs = (
        P(None, "azim", "section", "axial"),
        P(None, "azim", "section", "axial"),
        P("azim", "section", "axial"),
    )
    return jax.shard_map(functools.partial(body, sizes), mesh=mesh, in_specs=in_specs,
                         out_specs=out_specs, check_vma=False)
```

```python
import functools

import jax
import jax.numpy as jnp
from jax import lax
from jax.experimental import pallas as pl
from jax.experimental.pallas import tpu as pltpu
from jax.sharding import PartitionSpec as P

SWEEPS = 4
RIM = 8
MESH = pl.DeviceIdType.MESH


def pick(bits, table):
    low, mid, high = bits
    pairs = [jnp.where(low, table[2 * i + 1], table[2 * i]) for i in range(4)]
    return jnp.where(high, jnp.where(mid, pairs[3], pairs[2]), jnp.where(mid, pairs[1], pairs[0]))


def bits_of(regions):
    return ((regions & 1) != 0, (regions & 2) != 0, (regions & 4) != 0)


def kernel(sizes, *refs):
    S, N, C = sizes
    (A_hbm, J_hbm, fixed_hbm, spin_hbm, offs_hbm, *tables_hbm, prior, goal,
     misfit, dual, temp,
     turned, fixed, spin, offs, t_rel, t_eddy, t_loss, t_plane, t_axial, t_cap,
     AN, AX, AR, HN, HX, HR, regE, lossM, srcE, flux, H,
     priorX, goalX, regX, srcX, priorS, goalS, regS, srcS, priorP, goalP, regP, srcP,
     wa, wr, wl, inv, capH, rhsT, vT, vA, finT, finA, retA,
     A, J, relayG, relayP, local, send, recv) = refs
    R, L = fixed.shape
    rows = prior.shape[1]
    RROT = spin.shape[1]
    ext = rows + 2 * RIM
    s, j, c = lax.axis_index("section"), lax.axis_index("azim"), lax.axis_index("axial")
    Q = S * N
    q = s * N + j

    def section_id(d):
        return (lax.rem(s + d + S, S), j, c)

    def axial_id(d):
        return (s, j, lax.rem(c + d + C, C))

    def azim_id(d):
        return (s, lax.rem(j + d + N, N), c)

    barrier = pltpu.get_barrier_semaphore()
    partners = [azim_id(d) for d in range(1, N)]
    partners += [near(d) for near in (section_id, axial_id) for d in (1, -1)]
    for partner in partners:
        pl.semaphore_signal(barrier, inc=1, device_id=partner, device_id_type=MESH)

    loads = [
        pltpu.make_async_copy(A_hbm, A, local.at[0]),
        pltpu.make_async_copy(goal, goalX.at[:, pl.ds(RIM, rows), :], local.at[1]),
        pltpu.make_async_copy(prior, priorX.at[:, pl.ds(RIM, rows), :], local.at[2]),
        pltpu.make_async_copy(J_hbm, J, local.at[3]),
    ]
    tables = (t_rel, t_eddy, t_loss, t_plane, t_axial, t_cap)
    maps = [pltpu.make_async_copy(src, dst, local.at[4 + k]) for k, (src, dst) in enumerate(
        zip((fixed_hbm, spin_hbm, offs_hbm, *tables_hbm), (fixed, spin, offs, *tables)))]
    loads = maps + loads
    for load in loads:
        load.start()
    loads = loads[len(maps):]

    counter = [0]
    pending = []
    finals = []

    def slots(count):
        k = counter[0]
        counter[0] += count
        return k

    def remote(src, dst, device, k):
        return pltpu.make_async_remote_copy(
            src_ref=src, dst_ref=dst, send_sem=send.at[k], recv_sem=recv.at[k],
            device_id=device, device_id_type=MESH)

    def when(cond, f):
        if cond is None:
            f()
        else:
            pl.when(cond)(f)

    def unless(cond, f):
        when(None if cond is None else jnp.logical_not(cond), f)

    def copy(src, dst, device, sending=None, receiving=None):
        desc = remote(src, dst, device, slots(1))
        when(sending, lambda: desc.start())
        pending.append((desc, sending))
        return lambda: when(receiving, lambda: desc.wait_recv())

    def farthest(i):
        return jnp.where(j < N // 2, N - i, i)

    def both(*conds):
        return functools.reduce(jnp.logical_and, conds)

    top, bottom = j == 0, j == N - 1
    before, after = s > 0, s < S - 1

    up = lambda x, axis: pltpu.roll(x, x.shape[axis] - 1, axis)
    down = lambda x, axis: pltpu.roll(x, 1, axis)

    def each(f):
        if N <= 8:
            for a in range(N):
                f(a, (a + 1) % N, (a + N - 1) % N)
        else:
            def step(a, carry):
                f(a, lax.rem(a + 1, N), lax.rem(a + N - 1, N))
                return carry
            lax.fori_loop(0, N, step, 0)

    G = L // N
    assert G >= SWEEPS
    place = lax.broadcasted_iota(jnp.int32, (ext, L), 1) // G

    def forward(X, sides, packed):
        def add(a, ap, am):
            x = pltpu.roll(X[a], a * G, 1)
            first = isinstance(a, int) and a == 0
            packed[0] = x if first else jnp.where(place == a, x, packed[0])
            packed[1] = x if first else jnp.where(place == am, x, packed[1])
        each(add)
        return [copy(packed.at[0], sides.at[1], axial_id(-1), c > 0, c < C - 1),
                copy(packed.at[1], sides.at[0], axial_id(1), c < C - 1, c > 0)]

    def wide(X, sides, a):
        beside = jnp.where(place == a, sides[1], sides[0])
        return jnp.concatenate([X[a], pltpu.roll(beside, (L - a * G) % L, 1)], axis=1)

    def rims(src, X, relay):
        low, high = X.at[:, pl.ds(0, RIM), :], X.at[:, pl.ds(RIM + rows, RIM), :]
        first, last = src.at[:, 0:RIM, :], src.at[:, rows - RIM:rows, :]
        arrivals = [
            copy(last, low, azim_id(1), jnp.logical_not(bottom), jnp.logical_not(top)),
            copy(first, high, azim_id(-1), jnp.logical_not(top), jnp.logical_not(bottom))]
        down_hop = copy(last, relay.at[0], azim_id(1), both(bottom, after), both(top, after))
        up_hop = copy(first, relay.at[1], section_id(-1), both(top, before), both(top, after))

        def early():
            up_hop()
            arrivals.append(copy(relay.at[1], high, azim_id(-1), both(top, after), both(bottom, after)))

        def late():
            down_hop()
            arrivals.append(copy(relay.at[0], low, section_id(1), both(top, after), both(top, before)))
            return arrivals
        return early, late

    def spread(E, target, known=lambda peer: None):
        inner = ext - RIM

        def block(peer, slot, low, high, owner=j):
            first, count = (RIM if low else 0), (inner if low or high else ext)
            return remote(
                E.at[pl.ds(pl.multiple_of(peer * rows + first, 8), count), :],
                target.at[owner, pl.ds(first, count), :], (s, peer, c), slot)

        def cases(peer, f):
            pl.when(peer == 0)(lambda: f(True, False))
            pl.when(peer == N - 1)(lambda: f(False, True))
            pl.when(both(peer > 0, peer < N - 1))(lambda: f(False, False))

        k = slots(N - 1)
        for i in range(1, N):
            d = farthest(i)
            peer = lax.rem(j + d, N)
            unless(known(peer), lambda: cases(
                peer, lambda low, high: block(peer, k + d - 1, low, high).start()))
        for d in range(1, N):
            peer = lax.rem(j + d, N)
            finals.append(lambda peer=peer, d=d: unless(known(peer), lambda: cases(
                peer, lambda low, high: block(peer, k + d - 1, low, high).wait_send())))
        edges = [copy(E.at[R:R + RIM, :], E.at[0:RIM, :], section_id(1), after, before),
                 copy(E.at[RIM:2 * RIM, :], E.at[R + RIM:R + 2 * RIM, :], section_id(-1), before, after)]

        def rest():
            for arrive in edges:
                arrive()
            ends = []
            for peer, start, there in ((0, 0, before), (N - 1, RIM + rows, after)):
                b = slots(N - 1)
                d = lax.rem(peer - j + N, N)
                own = E.at[start if peer == 0 else R + RIM:(start if peer == 0 else R + RIM) + RIM, :]
                away = both(there, j != peer)
                desc = remote(own, target.at[j, pl.ds(start, RIM), :], (s, peer, c),
                              b + jnp.where(d > 0, d - 1, 0))
                pl.when(away)(lambda desc=desc: desc.start())
                pending.append((desc, away))
                for d in range(1, N):
                    got = remote(own, target.at[lax.rem(j - d + N, N), pl.ds(start, RIM), :],
                                 (s, peer, c), b + d - 1)
                    ends.append((got, both(there, j == peer)))
            target[j] = E[pl.ds(pl.multiple_of(j * rows, 8), ext), :]

            def arrived():
                for d in range(1, N):
                    owner = lax.rem(j - d + N, N)
                    unless(known(j), lambda: cases(
                        j, lambda low, high: block(j, k + d - 1, low, high, owner).wait_recv()))
                for got, here in ends:
                    pl.when(here)(lambda got=got: got.wait_recv())
            return arrived
        return rest

    pl.semaphore_wait(barrier, len(partners))

    got_an = copy(A_hbm.at[1:3], AN, azim_id(-1))
    got_ax = copy(A_hbm.at[0:2], AX, axial_id(-1), c > 0, c < C - 1)
    got_ar = copy(A_hbm.at[:, 0:RIM, :], AR, section_id(-1), before, after)

    for load in maps:
        load.wait()

    lane = lax.broadcasted_iota(jnp.int32, (R, L), 1)
    row = lax.broadcasted_iota(jnp.int32, (R, L), 0)
    for m in range(N):
        column = jnp.transpose(jnp.broadcast_to(spin[m:m + 1, :].astype(jnp.float32), (L, RROT)))
        turned[m, RIM:RIM + RROT, :] = column.astype(jnp.int32)

    def rotor(a, part, count):
        shift = a - offs[...]
        shift = jnp.broadcast_to(jnp.where(shift < 0, shift + N, shift), (count, L))
        value = turned[0, part, :]
        for m in range(1, N):
            value = jnp.where(shift == m, turned[m, part, :], value)
        return value

    def in_rotor(peer):
        return both(s == 0, (peer + 1) * rows + RIM <= RROT)

    regE[RIM:RIM + R, :] = fixed[...]
    regE[RIM:RIM + RROT, :] = jnp.where(s == 0, rotor(j, pl.ds(RIM, RROT), RROT), fixed[0:RROT, :])

    rest_reg = spread(regE, regX, in_rotor)
    goal_early, goal_late = rims(goal, goalX, relayG)
    prior_early, prior_late = rims(prior, priorX, relayP)
    lossM[...] = pick(bits_of(regE[RIM:RIM + R, :]), t_loss)
    got_reg = rest_reg()
    goal_early()
    prior_early()

    loads[0].wait()

    got_ax()
    got_ar()
    last_lane, last_row = c == C - 1, s == S - 1

    def lane_up(values, beside):
        beside = jnp.where(last_lane, 0.0, beside)
        return pltpu.roll(jnp.where(lane == 0, beside, values), L - 1, 1)

    def row_up(values, beside):
        beside = jnp.where(last_row, 0.0, beside)
        return jnp.where(row == R - 1, beside, pltpu.roll(values, R - 1, 0))

    flux[0] = (row_up(A[2], AR[2, 0:1, :]) - A[2]) - (lane_up(A[1], AX[1]) - A[1])
    flux[1] = lane_up(A[0], AX[0]) - A[0]
    flux[2] = A[0] - row_up(A[0], AR[0, 0:1, :])
    got_an()
    f0 = flux[0]
    f1 = flux[1] - (AN[1] - A[2])
    f2 = flux[2] + (AN[0] - A[1])
    flux[1] = f1
    flux[2] = f2
    srcE[RIM:RIM + R, :] = lossM[...] * (f0 * f0 + f1 * f1 + f2 * f2)
    rest_src = spread(srcE, srcX)
    reluct = pick(bits_of(regE[RIM:RIM + R, :]), t_rel)
    H[0] = reluct * flux[0]
    H[1] = reluct * flux[1]
    H[2] = reluct * flux[2]
    got_hr = copy(H.at[:, R - RIM:R, :], HR, section_id(1), after, before)
    got_src = rest_src()
    ring = [remote(H.at[1 + i // 1], HN.at[i // 1], azim_id(1), slots(1)) for i in range(2)]
    pending.extend((piece, None) for piece in ring)
    pl.when(both(j == N - 1, s == 0))(lambda: ring[0].start())
    pl.when(both(j == N - 1, s == 0))(lambda: ring[1].start())

    got_goal, got_prior = goal_late(), prior_late()

    got_reg()

    def own_rotor():
        def one(a, ap, am):
            regX[a] = rotor(a, pl.ds(pl.multiple_of(j * rows, 8), ext), ext)
        each(one)

    if RIM + rows <= RROT:
        pl.when(in_rotor(j))(own_rotor)
    got_reg = forward(regX, regS, regP)
    for load, arrivals in ((loads[1], got_goal), (loads[2], got_prior)):
        load.wait()
        for arrive in arrivals:
            arrive()
    got_goal = forward(goalX, goalS, goalP)
    got_prior = forward(priorX, priorS, priorP)

    got_src()
    got_src = forward(srcX, srcS, srcP)
    pl.when(j < N - 1)(lambda: ring[0].start())
    pl.when(both(j == N - 1, s > 0))(lambda: ring[0].start())
    pl.when(j < N - 1)(lambda: ring[1].start())
    got_hx = copy(H.at[0:2], HX, axial_id(1), c < C - 1, c > 0)

    def ext_mask():
        grow = lax.broadcasted_iota(jnp.int32, (ext, 2 * L), 0) + (q * rows - RIM)
        glane = lax.broadcasted_iota(jnp.int32, (ext, 2 * L), 1)
        ok = jnp.logical_and(grow >= 0, grow < Q * rows)
        right = jnp.logical_and(glane >= L, glane < L + L // 2)
        left = glane >= L + L // 2
        ok = jnp.logical_and(ok, jnp.logical_not(jnp.logical_and(right, c == C - 1)))
        return jnp.logical_and(ok, jnp.logical_not(jnp.logical_and(left, c == 0)))

    for arrive in got_reg:
        arrive()

    def first(a, ap, am):
        bits = bits_of(wide(regX, regS, a))
        ok = ext_mask()
        plane = jnp.where(ok, pick(bits, t_plane), 0.0)
        axial = jnp.where(ok, pick(bits, t_axial), 0.0)
        capH[a] = pick(bits, t_cap)
        inv[a] = plane
        wr[a] = 0.5 * (plane + up(plane, 0))
        wl[a] = 0.5 * (axial + up(axial, 1))

    def second(a, ap, am):
        wa[a] = 0.5 * (inv[a] + inv[ap])

    def third(a, ap, am):
        total = (wa[a] + wa[am]) + (wr[a] + down(wr[a], 0)) + (wl[a] + down(wl[a], 1)) + capH[a]
        inv[a] = jnp.where(ext_mask(), 1.0 / total, 0.0)

    each(first)
    each(second)
    each(third)

    def inflow(v, a, ap, am):
        x = v[a]
        r, l = wr[a], wl[a]
        return ((wa[a] * v[ap] + wa[am] * v[am]) + (r * up(x, 0) + down(r * x, 0))
                + (l * up(x, 1) + down(l * x, 1)))

    for arrive in got_goal:
        arrive()

    def adjoint_first(a, ap, am):
        rhs = jnp.where(ext_mask(), wide(goalX, goalS, a), 0.0)
        rhsT[a] = rhs
        vA[0, a] = rhs * inv[a]

    each(adjoint_first)

    def sweeps(v, count, final):
        for k in range(count):
            now, later = k % 2, (k + 1) % 2

            def one(a, ap, am):
                new = (rhsT[a] + inflow(v.at[now], a, ap, am)) * inv[a]
                if k == count - 1:
                    final[a] = new[RIM:RIM + rows, 0:L]
                else:
                    v[later, a] = new
            each(one)

    def gather(final, ret):
        k = slots(N - 1)

        def part(peer, slot, owner=j):
            return remote(final.at[peer], ret.at[pl.ds(pl.multiple_of(owner * rows, 8), rows), :],
                          (s, peer, c), slot)

        for i in range(1, N):
            d = farthest(i)
            peer = lax.rem(j + d, N)
            part(peer, k + d - 1).start()
        ret[pl.ds(pl.multiple_of(j * rows, 8), rows), :] = final[j]
        arrivals = []
        for d in range(1, N):
            pending.append((part(lax.rem(j + d, N), k + d - 1), None))
            owner = lax.rem(j - d + N, N)
            arrivals.append(lambda d=d, owner=owner: part(j, k + d - 1, owner).wait_recv())
        return arrivals

    sweeps(vA, SWEEPS - 1, finA)
    got_adj = gather(finA, retA)
    pl.when(both(j == N - 1, s > 0))(lambda: ring[1].start())

    for arrive in got_prior:
        arrive()
    for arrive in got_src:
        arrive()

    def thermal_first(a, ap, am):
        ok = ext_mask()
        start = jnp.where(ok, wide(priorX, priorS, a), 0.0)
        vT[0, a] = start
        rhsT[a] = capH[a] * start + jnp.where(ok, wide(srcX, srcS, a), 0.0)

    each(thermal_first)
    sweeps(vT, SWEEPS, finT)
    got_temp = gather(finT, temp)

    loads[3].wait()
    for piece in ring:
        piece.wait_recv()
    got_hx()
    got_hr()

    def lane_down(values, beside):
        beside = jnp.where(c == 0, 0.0, beside)
        return pltpu.roll(jnp.where(lane == L - 1, beside, values), 1, 1)

    def row_down(values, beside):
        beside = jnp.where(s == 0, 0.0, beside)
        return jnp.where(row == 0, beside, pltpu.roll(values, 1, 0))

    eddy = pick(bits_of(regE[RIM:RIM + R, :]), t_eddy)
    h0, h1, h2 = H[0], H[1], H[2]
    rim0, rim2 = HR[0, RIM - 1:RIM, :], HR[2, RIM - 1:RIM, :]
    misfit[0] = (lane_down(h1, HX[1]) - h1) - (row_down(h2, rim2) - h2) + eddy * A[0] - J[0]
    misfit[1] = (HN[1] - h2) - (lane_down(h0, HX[0]) - h0) + eddy * A[1] - J[1]
    misfit[2] = (row_down(h0, rim0) - h0) - (HN[0] - h1) + eddy * A[2] - J[2]

    for arrive in got_adj:
        arrive()
    scale = 2.0 * lossM[...] * retA[...]
    for k in range(3):
        dual[k] = scale * flux[k]
    for arrive in got_temp:
        arrive()
    for desc, sending in pending:
        when(sending, lambda: desc.wait_send())
    for final in finals:
        final()


def store(*refs):
    sems = refs[6]
    copies = [pltpu.make_async_copy(refs[k], refs[3 + k], sems.at[k]) for k in range(3)]
    for one in copies:
        one.start()
    for one in copies:
        one.wait()


def body(sizes, *args):
    (A, J, fixed, spin, offs, rel, eddy, loss, plane, axial, cap, prior, goal) = args
    _, one, R, L = A.shape
    assert one == 1 and spin.shape[1] <= R
    S, N, C = sizes
    rows = prior.shape[1]
    ext = rows + 2 * RIM
    f32 = jnp.float32
    vmem = pl.BlockSpec(memory_space=pltpu.VMEM)
    hbm = pl.BlockSpec(memory_space=pl.ANY)
    V = lambda *shape, dtype=f32: pltpu.VMEM(shape, dtype)
    copies = 48 + 8 * (N - 1)
    wide = (N, ext, 2 * L)
    misfit, dual, temp = pl.pallas_call(
        functools.partial(kernel, sizes),
        out_shape=(V(3, R, L), V(3, R, L), V(R, L)),
        in_specs=[hbm] * 13,
        out_specs=(vmem, vmem, vmem),
        scratch_shapes=[
            V(spin.shape[0], max(RIM + spin.shape[1], ext), L, dtype=jnp.int32),
            V(R, L, dtype=jnp.int32), V(*spin.shape, dtype=jnp.int32), V(1, L, dtype=jnp.int32),
            *[pltpu.SMEM(table.shape, f32) for table in (rel, eddy, loss, plane, axial, cap)],
            V(2, R, L), V(2, R, L), V(3, RIM, L), V(2, R, L), V(2, R, L), V(3, RIM, L),
            V(R + 2 * RIM, L, dtype=jnp.int32), V(R, L), V(R + 2 * RIM, L), V(3, R, L), V(3, R, L),
            V(N, ext, L), V(N, ext, L), V(N, ext, L, dtype=jnp.int32), V(N, ext, L),
            *[V(2, ext, L, dtype=kind) for kind in (f32, f32, jnp.int32, f32)] * 2,
            V(*wide), V(*wide), V(*wide), V(*wide), V(*wide), V(*wide), V(2, *wide), V(2, *wide),
            V(N, rows, L), V(N, rows, L), V(R, L), V(3, R, L), V(3, R, L),
            V(2, N, RIM, L), V(2, N, RIM, L), pltpu.SemaphoreType.DMA((13,)),
            pltpu.SemaphoreType.DMA((copies,)), pltpu.SemaphoreType.DMA((copies,)),
        ],
        compiler_params=pltpu.CompilerParams(collective_id=0, has_side_effects=True),
    )(A.reshape(3, R, L), J.reshape(3, R, L), fixed.reshape(R, L), spin, offs.reshape(1, L),
      rel, eddy, loss, plane, axial, cap, prior, goal)
    misfit, dual, temp = pl.pallas_call(
        store,
        out_shape=tuple(jax.ShapeDtypeStruct(x.shape, f32) for x in (misfit, dual, temp)),
        in_specs=[vmem] * 3,
        out_specs=(hbm, hbm, hbm),
        scratch_shapes=[pltpu.SemaphoreType.DMA((3,))],
    )(*(pltpu.with_memory_space_constraint(x, pltpu.VMEM) for x in (misfit, dual, temp)))
    return misfit.reshape(3, 1, R, L), dual.reshape(3, 1, R, L), temp.reshape(1, R, L)


def solution(mesh):
    sizes = (mesh.shape["section"], mesh.shape["azim"], mesh.shape["axial"])
    in_specs = (
        P(None, "azim", "section", "axial"),
        P(None, "azim", "section", "axial"),
        P("azim", "section", "axial"),
        P(),
        P("axial"),
        P(),
        P(),
        P(),
        P(),
        P(),
        P(),
        P(None, ("section", "azim"), "axial"),
        P(None, ("section", "azim"), "axial"),
    )
    out_specs = (
        P(None, "azim", "section", "axial"),
        P(None, "azim", "section", "axial"),
        P("azim", "section", "axial"),
    )
    return jax.shard_map(functools.partial(body, sizes), mesh=mesh, in_specs=in_specs,
                         out_specs=out_specs, check_vma=False)
```

```python
import functools

import jax
import jax.numpy as jnp
from jax import lax
from jax.experimental import pallas as pl
from jax.experimental.pallas import tpu as pltpu
from jax.sharding import PartitionSpec as P

SWEEPS = 4
RIM = 8
MESH = pl.DeviceIdType.MESH


def pick(bits, table):
    low, mid, high = bits
    pairs = [jnp.where(low, table[2 * i + 1], table[2 * i]) for i in range(4)]
    return jnp.where(high, jnp.where(mid, pairs[3], pairs[2]), jnp.where(mid, pairs[1], pairs[0]))


def bits_of(regions):
    return ((regions & 1) != 0, (regions & 2) != 0, (regions & 4) != 0)


def kernel(sizes, *refs):
    S, N, C = sizes
    (A_hbm, J_hbm, fixed_hbm, spin_hbm, offs_hbm, *tables_hbm, prior, goal,
     misfit, dual, temp,
     turned, fixed, spin, offs, t_rel, t_eddy, t_loss, t_plane, t_axial, t_cap,
     AN, AX, AR, HN, HX, HR, regE, lossM, srcE, flux, H,
     priorX, goalX, regX, srcX, priorS, goalS, regS, srcS, priorP, goalP, regP, srcP,
     wa, wr, wl, inv, capH, rhsT, vT, vA, finT, finA, retA,
     A, J, edge, beside, relay, local, send, recv) = refs
    R, L = fixed.shape
    rows = prior.shape[1]
    RROT = spin.shape[1]
    ext = rows + 2 * RIM
    s, j, c = lax.axis_index("section"), lax.axis_index("azim"), lax.axis_index("axial")
    Q = S * N
    q = s * N + j

    def section_id(d):
        return (lax.rem(s + d + S, S), j, c)

    def axial_id(d):
        return (s, j, lax.rem(c + d + C, C))

    def azim_id(d):
        return (s, lax.rem(j + d + N, N), c)

    barrier = pltpu.get_barrier_semaphore()
    partners = [azim_id(d) for d in range(1, N)]
    partners += [near(d) for near in (section_id, axial_id) for d in (1, -1)]
    for partner in partners:
        pl.semaphore_signal(barrier, inc=1, device_id=partner, device_id_type=MESH)

    loads = [
        pltpu.make_async_copy(A_hbm, A, local.at[0]),
        pltpu.make_async_copy(goal, goalX.at[:, pl.ds(RIM, rows), :], local.at[1]),
        pltpu.make_async_copy(prior, priorX.at[:, pl.ds(RIM, rows), :], local.at[2]),
        pltpu.make_async_copy(J_hbm, J, local.at[3]),
    ]
    tables = (t_rel, t_eddy, t_loss, t_plane, t_axial, t_cap)
    maps = [pltpu.make_async_copy(src, dst, local.at[4 + k]) for k, (src, dst) in enumerate(
        zip((fixed_hbm, spin_hbm, offs_hbm, *tables_hbm), (fixed, spin, offs, *tables)))]
    loads = maps + loads
    for load in loads:
        load.start()
    loads = loads[len(maps):]

    used = [0, 0]
    pending = []
    finals = []

    def slots(sends=1, receives=1):
        first = tuple(used)
        used[0] += sends
        used[1] += receives
        return first

    def remote(src, dst, device, slot, d=0):
        return pltpu.make_async_remote_copy(
            src_ref=src, dst_ref=dst, send_sem=send.at[slot[0] + d], recv_sem=recv.at[slot[1] + d],
            device_id=device, device_id_type=MESH)

    def when(cond, f):
        if cond is None:
            f()
        else:
            pl.when(cond)(f)

    def unless(cond, f):
        when(None if cond is None else jnp.logical_not(cond), f)

    def copy(src, dst, device, sending=None, receiving=None, slot=None):
        desc = remote(src, dst, device, slot or slots())
        when(sending, lambda: desc.start())
        pending.append((desc, sending))
        return lambda: when(receiving, lambda: desc.wait_recv())

    def farthest(i):
        return jnp.where(j < N // 2, N - i, i)

    def both(*conds):
        return functools.reduce(jnp.logical_and, conds)

    top, bottom = j == 0, j == N - 1
    before, after = s > 0, s < S - 1

    up = lambda x, axis: pltpu.roll(x, x.shape[axis] - 1, axis)
    down = lambda x, axis: pltpu.roll(x, 1, axis)

    def each(f):
        if N <= 8:
            for a in range(N):
                f(a, (a + 1) % N, (a + N - 1) % N)
        else:
            def step(a, carry):
                f(a, lax.rem(a + 1, N), lax.rem(a + N - 1, N))
                return carry
            lax.fori_loop(0, N, step, 0)

    G = L // N
    assert G >= SWEEPS
    place = lax.broadcasted_iota(jnp.int32, (ext, L), 1) // G

    def forward(X, sides, packed):
        def add(a, ap, am):
            x = pltpu.roll(X[a], a * G, 1)
            first = isinstance(a, int) and a == 0
            packed[0] = x if first else jnp.where(place == a, x, packed[0])
            packed[1] = x if first else jnp.where(place == am, x, packed[1])
        each(add)
        return [copy(packed.at[0], sides.at[1], axial_id(-1), c > 0, c < C - 1),
                copy(packed.at[1], sides.at[0], axial_id(1), c < C - 1, c > 0)]

    def wide(X, sides, a):
        beside = jnp.where(place == a, sides[1], sides[0])
        return jnp.concatenate([X[a], pltpu.roll(beside, (L - a * G) % L, 1)], axis=1)

    half = RIM // 2
    assert half >= SWEEPS

    def rims(edge, beside, relay):
        upper = lax.broadcasted_iota(jnp.int32, (RIM, L), 0) < half

        def cut(a, ap, am):
            def tile(X, first):
                return X[a, first:first + RIM, :]
            edge[0, a] = jnp.where(upper, pltpu.roll(tile(priorX, rows), half, 0), tile(goalX, rows))
            edge[1, a] = jnp.where(upper, tile(goalX, RIM), pltpu.roll(tile(priorX, RIM), half, 0))
        each(cut)
        low, high, last, first = beside.at[0], beside.at[1], edge.at[0], edge.at[1]
        (to_next, at_low), (to_last, at_high), (turn_low, at_first), (turn_high, at_second) = (
            slots() for _ in range(4))
        arrivals = [
            copy(last, low, azim_id(1), jnp.logical_not(bottom), jnp.logical_not(top), (to_next, at_low)),
            copy(first, high, azim_id(-1), jnp.logical_not(top), jnp.logical_not(bottom), (to_last, at_high))]
        down_hop = copy(last, relay.at[0], azim_id(1), both(bottom, after), both(top, after),
                        (to_next, at_first))
        up_hop = copy(first, relay.at[1], section_id(-1), both(top, before), both(top, after),
                      (to_last, at_second))

        def early():
            up_hop()
            arrivals.append(copy(relay.at[1], high, azim_id(-1), both(top, after), both(bottom, after),
                                 (turn_high, at_high)))

        def late():
            down_hop()
            arrivals.append(copy(relay.at[0], low, section_id(1), both(top, after), both(top, before),
                                 (turn_low, at_low)))

            def arrived():
                for arrive in arrivals:
                    arrive()

                def spread_rims(a, ap, am):
                    for k, first in ((0, 0), (1, RIM + rows)):
                        goalX[a, first:first + RIM, :] = beside[k, a]
                        priorX[a, first:first + RIM, :] = pltpu.roll(beside[k, a], half, 0)
                each(spread_rims)
            return arrived
        return early, late

    def spread(E, target, known=lambda peer: None):
        inner = ext - RIM

        def block(peer, d, low, high, owner=j):
            first, count = (RIM if low else 0), (inner if low or high else ext)
            return remote(
                E.at[pl.ds(pl.multiple_of(peer * rows + first, 8), count), :],
                target.at[owner, pl.ds(first, count), :], (s, peer, c), k, d - 1)

        def cases(peer, f):
            pl.when(peer == 0)(lambda: f(True, False))
            pl.when(peer == N - 1)(lambda: f(False, True))
            pl.when(both(peer > 0, peer < N - 1))(lambda: f(False, False))

        k = slots(N - 1, N - 1)
        for i in range(1, N):
            d = farthest(i)
            peer = lax.rem(j + d, N)
            unless(known(peer), lambda: cases(
                peer, lambda low, high: block(peer, d, low, high).start()))
        for d in range(1, N):
            peer = lax.rem(j + d, N)
            finals.append(lambda peer=peer, d=d: unless(known(peer), lambda: cases(
                peer, lambda low, high: block(peer, d, low, high).wait_send())))
        edges = [copy(E.at[R:R + RIM, :], E.at[0:RIM, :], section_id(1), after, before),
                 copy(E.at[RIM:2 * RIM, :], E.at[R + RIM:R + 2 * RIM, :], section_id(-1), before, after)]

        def rest():
            for arrive in edges:
                arrive()
            ends = []
            _, come = slots(0, N - 1)
            for peer, start, there in ((0, 0, before), (N - 1, RIM + rows, after)):
                go, _ = slots(1, 0)
                d = lax.rem(peer - j + N, N)
                own = E.at[start if peer == 0 else R + RIM:(start if peer == 0 else R + RIM) + RIM, :]
                away = both(there, j != peer)
                desc = remote(own, target.at[j, pl.ds(start, RIM), :], (s, peer, c),
                              (go, come + jnp.where(d > 0, d - 1, 0)))
                pl.when(away)(lambda desc=desc: desc.start())
                pending.append((desc, away))
                for d in range(1, N):
                    got = remote(own, target.at[lax.rem(j - d + N, N), pl.ds(start, RIM), :],
                                 (s, peer, c), (go, come + d - 1))
                    ends.append((got, both(there, j == peer)))
            target[j] = E[pl.ds(pl.multiple_of(j * rows, 8), ext), :]

            def arrived():
                for d in range(1, N):
                    owner = lax.rem(j - d + N, N)
                    unless(known(j), lambda: cases(
                        j, lambda low, high: block(j, d, low, high, owner).wait_recv()))
                for got, here in ends:
                    pl.when(here)(lambda got=got: got.wait_recv())
            return arrived
        return rest

    pl.semaphore_wait(barrier, len(partners))

    got_an = copy(A_hbm.at[1:3], AN, azim_id(-1))
    got_ax = copy(A_hbm.at[0:2], AX, axial_id(-1), c > 0, c < C - 1)
    got_ar = copy(A_hbm.at[:, 0:RIM, :], AR, section_id(-1), before, after)

    for load in maps:
        load.wait()

    lane = lax.broadcasted_iota(jnp.int32, (R, L), 1)
    row = lax.broadcasted_iota(jnp.int32, (R, L), 0)
    for m in range(N):
        column = jnp.transpose(jnp.broadcast_to(spin[m:m + 1, :].astype(jnp.float32), (L, RROT)))
        turned[m, RIM:RIM + RROT, :] = column.astype(jnp.int32)

    def rotor(a, part, count):
        shift = a - offs[...]
        shift = jnp.broadcast_to(jnp.where(shift < 0, shift + N, shift), (count, L))
        value = turned[0, part, :]
        for m in range(1, N):
            value = jnp.where(shift == m, turned[m, part, :], value)
        return value

    def in_rotor(peer):
        return both(s == 0, (peer + 1) * rows + RIM <= RROT)

    regE[RIM:RIM + R, :] = fixed[...]
    regE[RIM:RIM + RROT, :] = jnp.where(s == 0, rotor(j, pl.ds(RIM, RROT), RROT), fixed[0:RROT, :])

    rest_reg = spread(regE, regX, in_rotor)
    loads[1].wait()
    loads[2].wait()
    rims_early, rims_late = rims(edge, beside, relay)
    lossM[...] = pick(bits_of(regE[RIM:RIM + R, :]), t_loss)
    got_reg = rest_reg()
    rims_early()

    loads[0].wait()

    got_ax()
    got_ar()
    last_lane, last_row = c == C - 1, s == S - 1

    def lane_up(values, beside):
        beside = jnp.where(last_lane, 0.0, beside)
        return pltpu.roll(jnp.where(lane == 0, beside, values), L - 1, 1)

    def row_up(values, beside):
        beside = jnp.where(last_row, 0.0, beside)
        return jnp.where(row == R - 1, beside, pltpu.roll(values, R - 1, 0))

    flux[0] = (row_up(A[2], AR[2, 0:1, :]) - A[2]) - (lane_up(A[1], AX[1]) - A[1])
    flux[1] = lane_up(A[0], AX[0]) - A[0]
    flux[2] = A[0] - row_up(A[0], AR[0, 0:1, :])
    got_an()
    f0 = flux[0]
    f1 = flux[1] - (AN[1] - A[2])
    f2 = flux[2] + (AN[0] - A[1])
    flux[1] = f1
    flux[2] = f2
    srcE[RIM:RIM + R, :] = lossM[...] * (f0 * f0 + f1 * f1 + f2 * f2)
    rest_src = spread(srcE, srcX)
    reluct = pick(bits_of(regE[RIM:RIM + R, :]), t_rel)
    H[0] = reluct * flux[0]
    H[1] = reluct * flux[1]
    H[2] = reluct * flux[2]
    got_hr = copy(H.at[:, R - RIM:R, :], HR, section_id(1), after, before)
    got_src = rest_src()
    ring = [remote(H.at[1 + i // 1], HN.at[i // 1], azim_id(1), slots()) for i in range(2)]
    pending.extend((piece, None) for piece in ring)
    pl.when(both(j == N - 1, s == 0))(lambda: ring[0].start())
    pl.when(both(j == N - 1, s == 0))(lambda: ring[1].start())

    got_rims = rims_late()

    got_reg()

    def own_rotor():
        def one(a, ap, am):
            regX[a] = rotor(a, pl.ds(pl.multiple_of(j * rows, 8), ext), ext)
        each(one)

    if RIM + rows <= RROT:
        pl.when(in_rotor(j))(own_rotor)
    got_reg = forward(regX, regS, regP)
    got_rims()
    got_goal = forward(goalX, goalS, goalP)
    got_prior = forward(priorX, priorS, priorP)

    got_src()
    got_src = forward(srcX, srcS, srcP)
    pl.when(j < N - 1)(lambda: ring[0].start())
    pl.when(both(j == N - 1, s > 0))(lambda: ring[0].start())
    pl.when(j < N - 1)(lambda: ring[1].start())
    got_hx = copy(H.at[0:2], HX, axial_id(1), c < C - 1, c > 0)

    def ext_mask():
        grow = lax.broadcasted_iota(jnp.int32, (ext, 2 * L), 0) + (q * rows - RIM)
        glane = lax.broadcasted_iota(jnp.int32, (ext, 2 * L), 1)
        ok = jnp.logical_and(grow >= 0, grow < Q * rows)
        right = jnp.logical_and(glane >= L, glane < L + L // 2)
        left = glane >= L + L // 2
        ok = jnp.logical_and(ok, jnp.logical_not(jnp.logical_and(right, c == C - 1)))
        return jnp.logical_and(ok, jnp.logical_not(jnp.logical_and(left, c == 0)))

    for arrive in got_reg:
        arrive()

    def first(a, ap, am):
        bits = bits_of(wide(regX, regS, a))
        ok = ext_mask()
        plane = jnp.where(ok, pick(bits, t_plane), 0.0)
        axial = jnp.where(ok, pick(bits, t_axial), 0.0)
        capH[a] = pick(bits, t_cap)
        inv[a] = plane
        wr[a] = 0.5 * (plane + up(plane, 0))
        wl[a] = 0.5 * (axial + up(axial, 1))

    def second(a, ap, am):
        wa[a] = 0.5 * (inv[a] + inv[ap])

    def third(a, ap, am):
        total = (wa[a] + wa[am]) + (wr[a] + down(wr[a], 0)) + (wl[a] + down(wl[a], 1)) + capH[a]
        inv[a] = jnp.where(ext_mask(), 1.0 / total, 0.0)

    each(first)
    each(second)
    each(third)

    def inflow(v, a, ap, am):
        x = v[a]
        r, l = wr[a], wl[a]
        return ((wa[a] * v[ap] + wa[am] * v[am]) + (r * up(x, 0) + down(r * x, 0))
                + (l * up(x, 1) + down(l * x, 1)))

    for arrive in got_goal:
        arrive()

    def adjoint_first(a, ap, am):
        rhs = jnp.where(ext_mask(), wide(goalX, goalS, a), 0.0)
        rhsT[a] = rhs
        vA[0, a] = rhs * inv[a]

    each(adjoint_first)

    def sweeps(v, count, final):
        for k in range(count):
            now, later = k % 2, (k + 1) % 2

            def one(a, ap, am):
                new = (rhsT[a] + inflow(v.at[now], a, ap, am)) * inv[a]
                if k == count - 1:
                    final[a] = new[RIM:RIM + rows, 0:L]
                else:
                    v[later, a] = new
            each(one)

    def gather(final, ret):
        k = slots(N - 1, N - 1)

        def part(peer, d, owner=j):
            return remote(final.at[peer], ret.at[pl.ds(pl.multiple_of(owner * rows, 8), rows), :],
                          (s, peer, c), k, d - 1)

        for i in range(1, N):
            d = farthest(i)
            peer = lax.rem(j + d, N)
            part(peer, d).start()
        ret[pl.ds(pl.multiple_of(j * rows, 8), rows), :] = final[j]
        arrivals = []
        for d in range(1, N):
            pending.append((part(lax.rem(j + d, N), d), None))
            owner = lax.rem(j - d + N, N)
            arrivals.append(lambda d=d, owner=owner: part(j, d, owner).wait_recv())
        return arrivals

    sweeps(vA, SWEEPS - 1, finA)
    got_adj = gather(finA, retA)
    pl.when(both(j == N - 1, s > 0))(lambda: ring[1].start())

    for arrive in got_prior:
        arrive()
    for arrive in got_src:
        arrive()

    def thermal_first(a, ap, am):
        ok = ext_mask()
        start = jnp.where(ok, wide(priorX, priorS, a), 0.0)
        vT[0, a] = start
        rhsT[a] = capH[a] * start + jnp.where(ok, wide(srcX, srcS, a), 0.0)

    each(thermal_first)
    sweeps(vT, SWEEPS, finT)
    got_temp = gather(finT, temp)

    loads[3].wait()
    for piece in ring:
        piece.wait_recv()
    got_hx()
    got_hr()

    def lane_down(values, beside):
        beside = jnp.where(c == 0, 0.0, beside)
        return pltpu.roll(jnp.where(lane == L - 1, beside, values), 1, 1)

    def row_down(values, beside):
        beside = jnp.where(s == 0, 0.0, beside)
        return jnp.where(row == 0, beside, pltpu.roll(values, 1, 0))

    eddy = pick(bits_of(regE[RIM:RIM + R, :]), t_eddy)
    h0, h1, h2 = H[0], H[1], H[2]
    rim0, rim2 = HR[0, RIM - 1:RIM, :], HR[2, RIM - 1:RIM, :]
    misfit[0] = (lane_down(h1, HX[1]) - h1) - (row_down(h2, rim2) - h2) + eddy * A[0] - J[0]
    misfit[1] = (HN[1] - h2) - (lane_down(h0, HX[0]) - h0) + eddy * A[1] - J[1]
    misfit[2] = (row_down(h0, rim0) - h0) - (HN[0] - h1) + eddy * A[2] - J[2]

    for arrive in got_adj:
        arrive()
    scale = 2.0 * lossM[...] * retA[...]
    for k in range(3):
        dual[k] = scale * flux[k]
    for arrive in got_temp:
        arrive()
    for desc, sending in pending:
        when(sending, lambda: desc.wait_send())
    for final in finals:
        final()
    assert used == [send.shape[0], recv.shape[0]]


def store(*refs):
    sems = refs[6]
    copies = [pltpu.make_async_copy(refs[k], refs[3 + k], sems.at[k]) for k in range(3)]
    for one in copies:
        one.start()
    for one in copies:
        one.wait()


def body(sizes, *args):
    (A, J, fixed, spin, offs, rel, eddy, loss, plane, axial, cap, prior, goal) = args
    _, one, R, L = A.shape
    assert one == 1 and spin.shape[1] <= R
    S, N, C = sizes
    rows = prior.shape[1]
    ext = rows + 2 * RIM
    f32 = jnp.float32
    vmem = pl.BlockSpec(memory_space=pltpu.VMEM)
    hbm = pl.BlockSpec(memory_space=pl.ANY)
    V = lambda *shape, dtype=f32: pltpu.VMEM(shape, dtype)
    wide = (N, ext, 2 * L)
    misfit, dual, temp = pl.pallas_call(
        functools.partial(kernel, sizes),
        out_shape=(V(3, R, L), V(3, R, L), V(R, L)),
        in_specs=[hbm] * 13,
        out_specs=(vmem, vmem, vmem),
        scratch_shapes=[
            V(spin.shape[0], max(RIM + spin.shape[1], ext), L, dtype=jnp.int32),
            V(R, L, dtype=jnp.int32), V(*spin.shape, dtype=jnp.int32), V(1, L, dtype=jnp.int32),
            *[pltpu.SMEM(table.shape, f32) for table in (rel, eddy, loss, plane, axial, cap)],
            V(2, R, L), V(2, R, L), V(3, RIM, L), V(2, R, L), V(2, R, L), V(3, RIM, L),
            V(R + 2 * RIM, L, dtype=jnp.int32), V(R, L), V(R + 2 * RIM, L), V(3, R, L), V(3, R, L),
            V(N, ext, L), V(N, ext, L), V(N, ext, L, dtype=jnp.int32), V(N, ext, L),
            *[V(2, ext, L, dtype=kind) for kind in (f32, f32, jnp.int32, f32)] * 2,
            V(*wide), V(*wide), V(*wide), V(*wide), V(*wide), V(*wide), V(2, *wide), V(2, *wide),
            V(N, rows, L), V(N, rows, L), V(R, L), V(3, R, L), V(3, R, L),
            V(2, N, RIM, L), V(2, N, RIM, L), V(2, N, RIM, L), pltpu.SemaphoreType.DMA((13,)),
            pltpu.SemaphoreType.DMA((27 + 4 * (N - 1),)), pltpu.SemaphoreType.DMA((23 + 6 * (N - 1),)),
        ],
        compiler_params=pltpu.CompilerParams(collective_id=0, has_side_effects=True),
    )(A.reshape(3, R, L), J.reshape(3, R, L), fixed.reshape(R, L), spin, offs.reshape(1, L),
      rel, eddy, loss, plane, axial, cap, prior, goal)
    misfit, dual, temp = pl.pallas_call(
        store,
        out_shape=tuple(jax.ShapeDtypeStruct(x.shape, f32) for x in (misfit, dual, temp)),
        in_specs=[vmem] * 3,
        out_specs=(hbm, hbm, hbm),
        scratch_shapes=[pltpu.SemaphoreType.DMA((3,))],
    )(*(pltpu.with_memory_space_constraint(x, pltpu.VMEM) for x in (misfit, dual, temp)))
    return misfit.reshape(3, 1, R, L), dual.reshape(3, 1, R, L), temp.reshape(1, R, L)


def solution(mesh):
    sizes = (mesh.shape["section"], mesh.shape["azim"], mesh.shape["axial"])
    in_specs = (
        P(None, "azim", "section", "axial"),
        P(None, "azim", "section", "axial"),
        P("azim", "section", "axial"),
        P(),
        P("axial"),
        P(),
        P(),
        P(),
        P(),
        P(),
        P(),
        P(None, ("section", "azim"), "axial"),
        P(None, ("section", "azim"), "axial"),
    )
    out_specs = (
        P(None, "azim", "section", "axial"),
        P(None, "azim", "section", "axial"),
        P("azim", "section", "axial"),
    )
    return jax.shard_map(functools.partial(body, sizes), mesh=mesh, in_specs=in_specs,
                         out_specs=out_specs, check_vma=False)
```

```python
import functools

import jax
import jax.numpy as jnp
from jax import lax
from jax.experimental import pallas as pl
from jax.experimental.pallas import tpu as pltpu
from jax.sharding import PartitionSpec as P

SWEEPS = 4
RIM = 8
MESH = pl.DeviceIdType.MESH


def pick(bits, table):
    low, mid, high = bits
    pairs = [jnp.where(low, table[2 * i + 1], table[2 * i]) for i in range(4)]
    return jnp.where(high, jnp.where(mid, pairs[3], pairs[2]), jnp.where(mid, pairs[1], pairs[0]))


def bits_of(regions):
    return ((regions & 1) != 0, (regions & 2) != 0, (regions & 4) != 0)


def kernel(sizes, *refs):
    S, N, C = sizes
    (A_hbm, J_hbm, fixed_hbm, spin_hbm, offs_hbm, *tables_hbm, prior, goal,
     misfit, dual, temp,
     turned, fixed, spin, offs, t_rel, t_eddy, t_loss, t_plane, t_axial, t_cap,
     AN, AX, AR, HN, HX, HR, regE, lossM, srcE, flux, H,
     priorX, goalX, regX, srcX, priorS, goalS, regS, srcS, priorP, goalP, regP, srcP,
     wa, wr, wl, inv, capH, rhsT, vT, vA, finT, finA, retA,
     A, J, edge, beside, relay, local, send, recv) = refs
    R, L = fixed.shape
    rows = prior.shape[1]
    RROT = spin.shape[1]
    ext = rows + 2 * RIM
    s, j, c = lax.axis_index("section"), lax.axis_index("azim"), lax.axis_index("axial")
    Q = S * N
    q = s * N + j

    def section_id(d):
        return (lax.rem(s + d + S, S), j, c)

    def axial_id(d):
        return (s, j, lax.rem(c + d + C, C))

    def azim_id(d):
        return (s, lax.rem(j + d + N, N), c)

    barrier = pltpu.get_barrier_semaphore()
    partners = [azim_id(d) for d in range(1, N)]
    partners += [near(d) for near in (section_id, axial_id) for d in (1, -1)]
    for partner in partners:
        pl.semaphore_signal(barrier, inc=1, device_id=partner, device_id_type=MESH)

    loads = [
        pltpu.make_async_copy(A_hbm, A, local.at[0]),
        pltpu.make_async_copy(goal, goalX.at[:, pl.ds(RIM, rows), :], local.at[1]),
        pltpu.make_async_copy(prior, priorX.at[:, pl.ds(RIM, rows), :], local.at[2]),
        pltpu.make_async_copy(J_hbm, J, local.at[3]),
    ]
    tables = (t_rel, t_eddy, t_loss, t_plane, t_axial, t_cap)
    maps = [pltpu.make_async_copy(src, dst, local.at[4 + k]) for k, (src, dst) in enumerate(
        zip((fixed_hbm, spin_hbm, offs_hbm, *tables_hbm), (fixed, spin, offs, *tables)))]
    loads = maps + loads
    for load in loads:
        load.start()
    loads = loads[len(maps):]

    used = [0, 0]
    pending = []
    finals = []

    def slots(sends=1, receives=1):
        first = tuple(used)
        used[0] += sends
        used[1] += receives
        return first

    def remote(src, dst, device, slot, d=0):
        return pltpu.make_async_remote_copy(
            src_ref=src, dst_ref=dst, send_sem=send.at[slot[0] + d], recv_sem=recv.at[slot[1] + d],
            device_id=device, device_id_type=MESH)

    def when(cond, f):
        if cond is None:
            f()
        else:
            pl.when(cond)(f)

    def unless(cond, f):
        when(None if cond is None else jnp.logical_not(cond), f)

    def copy(src, dst, device, sending=None, receiving=None, slot=None):
        desc = remote(src, dst, device, slot or slots())
        when(sending, lambda: desc.start())
        pending.append((desc, sending))
        return lambda: when(receiving, lambda: desc.wait_recv())

    def farthest(i):
        return jnp.where(j < N // 2, N - i, i)

    def both(*conds):
        return functools.reduce(jnp.logical_and, conds)

    top, bottom = j == 0, j == N - 1
    before, after = s > 0, s < S - 1

    up = lambda x, axis: pltpu.roll(x, x.shape[axis] - 1, axis)
    down = lambda x, axis: pltpu.roll(x, 1, axis)

    def each(f):
        if N <= 8:
            for a in range(N):
                f(a, (a + 1) % N, (a + N - 1) % N)
        else:
            def step(a, carry):
                f(a, lax.rem(a + 1, N), lax.rem(a + N - 1, N))
                return carry
            lax.fori_loop(0, N, step, 0)

    G = L // N
    assert G >= SWEEPS
    place = lax.broadcasted_iota(jnp.int32, (ext, L), 1) // G

    def forward(X, sides, packed):
        def add(a, ap, am):
            x = pltpu.roll(X[a], a * G, 1)
            first = isinstance(a, int) and a == 0
            packed[0] = x if first else jnp.where(place == a, x, packed[0])
            packed[1] = x if first else jnp.where(place == am, x, packed[1])
        each(add)
        return [copy(packed.at[0], sides.at[1], axial_id(-1), c > 0, c < C - 1),
                copy(packed.at[1], sides.at[0], axial_id(1), c < C - 1, c > 0)]

    def wide(X, sides, a):
        beside = jnp.where(place == a, sides[1], sides[0])
        return jnp.concatenate([X[a], pltpu.roll(beside, (L - a * G) % L, 1)], axis=1)

    half = RIM // 2
    assert half >= SWEEPS

    def rims(edge, beside, relay):
        upper = lax.broadcasted_iota(jnp.int32, (RIM, L), 0) < half

        def cut(a, ap, am):
            def tile(X, first):
                return X[a, first:first + RIM, :]
            edge[0, a] = jnp.where(upper, pltpu.roll(tile(priorX, rows), half, 0), tile(goalX, rows))
            edge[1, a] = jnp.where(upper, tile(goalX, RIM), pltpu.roll(tile(priorX, RIM), half, 0))
        each(cut)
        low, high, last, first = beside.at[0], beside.at[1], edge.at[0], edge.at[1]
        (to_next, at_low), (to_last, at_high), (turn_low, at_first), (turn_high, at_second) = (
            slots() for _ in range(4))
        arrivals = [
            copy(last, low, azim_id(1), jnp.logical_not(bottom), jnp.logical_not(top), (to_next, at_low)),
            copy(first, high, azim_id(-1), jnp.logical_not(top), jnp.logical_not(bottom), (to_last, at_high))]
        down_hop = copy(last, relay.at[0], azim_id(1), both(bottom, after), both(top, after),
                        (to_next, at_first))
        up_hop = copy(first, relay.at[1], section_id(-1), both(top, before), both(top, after),
                      (to_last, at_second))

        def early():
            up_hop()
            arrivals.append(copy(relay.at[1], high, azim_id(-1), both(top, after), both(bottom, after),
                                 (turn_high, at_high)))

        def late():
            down_hop()
            arrivals.append(copy(relay.at[0], low, section_id(1), both(top, after), both(top, before),
                                 (turn_low, at_low)))

            def arrived():
                for arrive in arrivals:
                    arrive()

                def spread_rims(a, ap, am):
                    for k, first in ((0, 0), (1, RIM + rows)):
                        goalX[a, first:first + RIM, :] = beside[k, a]
                        priorX[a, first:first + RIM, :] = pltpu.roll(beside[k, a], half, 0)
                each(spread_rims)
            return arrived
        return early, late

    def spread(E, target, known=lambda peer: None):
        inner = ext - RIM

        def block(peer, d, low, high, owner=j):
            first, count = (RIM if low else 0), (inner if low or high else ext)
            return remote(
                E.at[pl.ds(pl.multiple_of(peer * rows + first, 8), count), :],
                target.at[owner, pl.ds(first, count), :], (s, peer, c), k, d - 1)

        def cases(peer, f):
            pl.when(peer == 0)(lambda: f(True, False))
            pl.when(peer == N - 1)(lambda: f(False, True))
            pl.when(both(peer > 0, peer < N - 1))(lambda: f(False, False))

        k = slots(N - 1, N - 1)
        for i in range(1, N):
            d = farthest(i)
            peer = lax.rem(j + d, N)
            unless(known(peer), lambda: cases(
                peer, lambda low, high: block(peer, d, low, high).start()))
        for d in range(1, N):
            peer = lax.rem(j + d, N)
            finals.append(lambda peer=peer, d=d: unless(known(peer), lambda: cases(
                peer, lambda low, high: block(peer, d, low, high).wait_send())))
        edges = [copy(E.at[R:R + RIM, :], E.at[0:RIM, :], section_id(1), after, before),
                 copy(E.at[RIM:2 * RIM, :], E.at[R + RIM:R + 2 * RIM, :], section_id(-1), before, after)]

        def rest():
            for arrive in edges:
                arrive()
            ends = []
            _, come = slots(0, N - 1)
            for peer, start, there in ((0, 0, before), (N - 1, RIM + rows, after)):
                go, _ = slots(1, 0)
                d = lax.rem(peer - j + N, N)
                own = E.at[start if peer == 0 else R + RIM:(start if peer == 0 else R + RIM) + RIM, :]
                away = both(there, j != peer)
                desc = remote(own, target.at[j, pl.ds(start, RIM), :], (s, peer, c),
                              (go, come + jnp.where(d > 0, d - 1, 0)))
                pl.when(away)(lambda desc=desc: desc.start())
                pending.append((desc, away))
                for d in range(1, N):
                    got = remote(own, target.at[lax.rem(j - d + N, N), pl.ds(start, RIM), :],
                                 (s, peer, c), (go, come + d - 1))
                    ends.append((got, both(there, j == peer)))
            target[j] = E[pl.ds(pl.multiple_of(j * rows, 8), ext), :]

            def arrived():
                for d in range(1, N):
                    owner = lax.rem(j - d + N, N)
                    unless(known(j), lambda: cases(
                        j, lambda low, high: block(j, d, low, high, owner).wait_recv()))
                for got, here in ends:
                    pl.when(here)(lambda got=got: got.wait_recv())
            return arrived
        return rest

    pl.semaphore_wait(barrier, len(partners))

    got_an = copy(A_hbm.at[1:3], AN, azim_id(-1))
    got_ax = copy(A_hbm.at[0:2], AX, axial_id(-1), c > 0, c < C - 1)
    got_ar = copy(A_hbm.at[:, 0:RIM, :], AR, section_id(-1), before, after)

    for load in maps:
        load.wait()

    lane = lax.broadcasted_iota(jnp.int32, (R, L), 1)
    row = lax.broadcasted_iota(jnp.int32, (R, L), 0)
    for m in range(N):
        column = jnp.transpose(jnp.broadcast_to(spin[m:m + 1, :].astype(jnp.float32), (L, RROT)))
        turned[m, RIM:RIM + RROT, :] = column.astype(jnp.int32)

    def rotor(a, part, count):
        shift = a - offs[...]
        shift = jnp.broadcast_to(jnp.where(shift < 0, shift + N, shift), (count, L))
        value = turned[0, part, :]
        for m in range(1, N):
            value = jnp.where(shift == m, turned[m, part, :], value)
        return value

    def in_rotor(peer):
        return both(s == 0, (peer + 1) * rows + RIM <= RROT)

    regE[RIM:RIM + R, :] = fixed[...]
    regE[RIM:RIM + RROT, :] = jnp.where(s == 0, rotor(j, pl.ds(RIM, RROT), RROT), fixed[0:RROT, :])

    rest_reg = spread(regE, regX, in_rotor)
    loads[1].wait()
    loads[2].wait()
    rims_early, rims_late = rims(edge, beside, relay)
    lossM[...] = pick(bits_of(regE[RIM:RIM + R, :]), t_loss)
    got_reg = rest_reg()
    rims_early()

    loads[0].wait()

    got_ax()
    got_ar()
    last_lane, last_row = c == C - 1, s == S - 1

    def lane_up(values, beside):
        beside = jnp.where(last_lane, 0.0, beside)
        return pltpu.roll(jnp.where(lane == 0, beside, values), L - 1, 1)

    def row_up(values, beside):
        beside = jnp.where(last_row, 0.0, beside)
        return jnp.where(row == R - 1, beside, pltpu.roll(values, R - 1, 0))

    flux[0] = (row_up(A[2], AR[2, 0:1, :]) - A[2]) - (lane_up(A[1], AX[1]) - A[1])
    flux[1] = lane_up(A[0], AX[0]) - A[0]
    flux[2] = A[0] - row_up(A[0], AR[0, 0:1, :])
    got_an()
    f0 = flux[0]
    f1 = flux[1] - (AN[1] - A[2])
    f2 = flux[2] + (AN[0] - A[1])
    flux[1] = f1
    flux[2] = f2
    srcE[RIM:RIM + R, :] = lossM[...] * (f0 * f0 + f1 * f1 + f2 * f2)
    rest_src = spread(srcE, srcX)
    reluct = pick(bits_of(regE[RIM:RIM + R, :]), t_rel)
    H[0] = reluct * flux[0]
    H[1] = reluct * flux[1]
    H[2] = reluct * flux[2]
    got_hr = copy(H.at[:, R - RIM:R, :], HR, section_id(1), after, before)
    got_src = rest_src()
    ring = [remote(H.at[1 + i // 1], HN.at[i // 1], azim_id(1), slots()) for i in range(2)]
    pending.extend((piece, None) for piece in ring)
    pl.when(both(j == N - 1, s == 0))(lambda: ring[0].start())
    pl.when(both(j == N - 1, s == 0))(lambda: ring[1].start())

    got_rims = rims_late()

    got_reg()

    def own_rotor():
        def one(a, ap, am):
            regX[a] = rotor(a, pl.ds(pl.multiple_of(j * rows, 8), ext), ext)
        each(one)

    if RIM + rows <= RROT:
        pl.when(in_rotor(j))(own_rotor)
    got_reg = forward(regX, regS, regP)
    got_rims()
    pl.when(both(j == N - 1, s > 0, c % 2 == 0))(lambda: ring[0].start())
    pl.when(both(j < N - 1, c % 2 == 0))(lambda: ring[0].start())
    got_goal = forward(goalX, goalS, goalP)
    got_prior = forward(priorX, priorS, priorP)

    got_src()
    got_src = forward(srcX, srcS, srcP)
    pl.when(both(j == N - 1, s > 0, c % 2 == 1))(lambda: ring[0].start())
    pl.when(both(j < N - 1, c % 2 == 1))(lambda: ring[0].start())
    pl.when(j < N - 1)(lambda: ring[1].start())
    got_hx = copy(H.at[0:2], HX, axial_id(1), c < C - 1, c > 0)

    def ext_mask():
        grow = lax.broadcasted_iota(jnp.int32, (ext, 2 * L), 0) + (q * rows - RIM)
        glane = lax.broadcasted_iota(jnp.int32, (ext, 2 * L), 1)
        ok = jnp.logical_and(grow >= 0, grow < Q * rows)
        right = jnp.logical_and(glane >= L, glane < L + L // 2)
        left = glane >= L + L // 2
        ok = jnp.logical_and(ok, jnp.logical_not(jnp.logical_and(right, c == C - 1)))
        return jnp.logical_and(ok, jnp.logical_not(jnp.logical_and(left, c == 0)))

    for arrive in got_reg:
        arrive()

    def first(a, ap, am):
        bits = bits_of(wide(regX, regS, a))
        ok = ext_mask()
        plane = jnp.where(ok, pick(bits, t_plane), 0.0)
        axial = jnp.where(ok, pick(bits, t_axial), 0.0)
        capH[a] = pick(bits, t_cap)
        inv[a] = plane
        wr[a] = 0.5 * (plane + up(plane, 0))
        wl[a] = 0.5 * (axial + up(axial, 1))

    def second(a, ap, am):
        wa[a] = 0.5 * (inv[a] + inv[ap])

    def third(a, ap, am):
        total = (wa[a] + wa[am]) + (wr[a] + down(wr[a], 0)) + (wl[a] + down(wl[a], 1)) + capH[a]
        inv[a] = jnp.where(ext_mask(), 1.0 / total, 0.0)

    each(first)
    each(second)
    each(third)

    def inflow(v, a, ap, am):
        x = v[a]
        r, l = wr[a], wl[a]
        return ((wa[a] * v[ap] + wa[am] * v[am]) + (r * up(x, 0) + down(r * x, 0))
                + (l * up(x, 1) + down(l * x, 1)))

    for arrive in got_goal:
        arrive()

    def adjoint_first(a, ap, am):
        rhs = jnp.where(ext_mask(), wide(goalX, goalS, a), 0.0)
        rhsT[a] = rhs
        vA[0, a] = rhs * inv[a]

    each(adjoint_first)

    def sweeps(v, count, final):
        for k in range(count):
            now, later = k % 2, (k + 1) % 2

            def one(a, ap, am):
                new = (rhsT[a] + inflow(v.at[now], a, ap, am)) * inv[a]
                if k == count - 1:
                    final[a] = new[RIM:RIM + rows, 0:L]
                else:
                    v[later, a] = new
            each(one)

    def gather(final, ret):
        k = slots(N - 1, N - 1)

        def part(peer, d, owner=j):
            return remote(final.at[peer], ret.at[pl.ds(pl.multiple_of(owner * rows, 8), rows), :],
                          (s, peer, c), k, d - 1)

        for i in range(1, N):
            d = farthest(i)
            peer = lax.rem(j + d, N)
            part(peer, d).start()
        ret[pl.ds(pl.multiple_of(j * rows, 8), rows), :] = final[j]
        arrivals = []
        for d in range(1, N):
            pending.append((part(lax.rem(j + d, N), d), None))
            owner = lax.rem(j - d + N, N)
            arrivals.append(lambda d=d, owner=owner: part(j, d, owner).wait_recv())
        return arrivals

    sweeps(vA, SWEEPS - 1, finA)
    got_adj = gather(finA, retA)
    pl.when(both(j == N - 1, s > 0))(lambda: ring[1].start())

    for arrive in got_prior:
        arrive()
    for arrive in got_src:
        arrive()

    def thermal_first(a, ap, am):
        ok = ext_mask()
        start = jnp.where(ok, wide(priorX, priorS, a), 0.0)
        vT[0, a] = start
        rhsT[a] = capH[a] * start + jnp.where(ok, wide(srcX, srcS, a), 0.0)

    each(thermal_first)
    sweeps(vT, SWEEPS, finT)
    got_temp = gather(finT, temp)

    loads[3].wait()
    for piece in ring:
        piece.wait_recv()
    got_hx()
    got_hr()

    def lane_down(values, beside):
        beside = jnp.where(c == 0, 0.0, beside)
        return pltpu.roll(jnp.where(lane == L - 1, beside, values), 1, 1)

    def row_down(values, beside):
        beside = jnp.where(s == 0, 0.0, beside)
        return jnp.where(row == 0, beside, pltpu.roll(values, 1, 0))

    eddy = pick(bits_of(regE[RIM:RIM + R, :]), t_eddy)
    h0, h1, h2 = H[0], H[1], H[2]
    rim0, rim2 = HR[0, RIM - 1:RIM, :], HR[2, RIM - 1:RIM, :]
    misfit[0] = (lane_down(h1, HX[1]) - h1) - (row_down(h2, rim2) - h2) + eddy * A[0] - J[0]
    misfit[1] = (HN[1] - h2) - (lane_down(h0, HX[0]) - h0) + eddy * A[1] - J[1]
    misfit[2] = (row_down(h0, rim0) - h0) - (HN[0] - h1) + eddy * A[2] - J[2]

    for arrive in got_adj:
        arrive()
    scale = 2.0 * lossM[...] * retA[...]
    for k in range(3):
        dual[k] = scale * flux[k]
    for arrive in got_temp:
        arrive()
    for desc, sending in pending:
        when(sending, lambda: desc.wait_send())
    for final in finals:
        final()
    assert used == [send.shape[0], recv.shape[0]]


def store(*refs):
    sems = refs[6]
    copies = [pltpu.make_async_copy(refs[k], refs[3 + k], sems.at[k]) for k in range(3)]
    for one in copies:
        one.start()
    for one in copies:
        one.wait()


def body(sizes, *args):
    (A, J, fixed, spin, offs, rel, eddy, loss, plane, axial, cap, prior, goal) = args
    _, one, R, L = A.shape
    assert one == 1 and spin.shape[1] <= R
    S, N, C = sizes
    rows = prior.shape[1]
    ext = rows + 2 * RIM
    f32 = jnp.float32
    vmem = pl.BlockSpec(memory_space=pltpu.VMEM)
    hbm = pl.BlockSpec(memory_space=pl.ANY)
    V = lambda *shape, dtype=f32: pltpu.VMEM(shape, dtype)
    wide = (N, ext, 2 * L)
    misfit, dual, temp = pl.pallas_call(
        functools.partial(kernel, sizes),
        out_shape=(V(3, R, L), V(3, R, L), V(R, L)),
        in_specs=[hbm] * 13,
        out_specs=(vmem, vmem, vmem),
        scratch_shapes=[
            V(spin.shape[0], max(RIM + spin.shape[1], ext), L, dtype=jnp.int32),
            V(R, L, dtype=jnp.int32), V(*spin.shape, dtype=jnp.int32), V(1, L, dtype=jnp.int32),
            *[pltpu.SMEM(table.shape, f32) for table in (rel, eddy, loss, plane, axial, cap)],
            V(2, R, L), V(2, R, L), V(3, RIM, L), V(2, R, L), V(2, R, L), V(3, RIM, L),
            V(R + 2 * RIM, L, dtype=jnp.int32), V(R, L), V(R + 2 * RIM, L), V(3, R, L), V(3, R, L),
            V(N, ext, L), V(N, ext, L), V(N, ext, L, dtype=jnp.int32), V(N, ext, L),
            *[V(2, ext, L, dtype=kind) for kind in (f32, f32, jnp.int32, f32)] * 2,
            V(*wide), V(*wide), V(*wide), V(*wide), V(*wide), V(*wide), V(2, *wide), V(2, *wide),
            V(N, rows, L), V(N, rows, L), V(R, L), V(3, R, L), V(3, R, L),
            V(2, N, RIM, L), V(2, N, RIM, L), V(2, N, RIM, L), pltpu.SemaphoreType.DMA((13,)),
            pltpu.SemaphoreType.DMA((27 + 4 * (N - 1),)), pltpu.SemaphoreType.DMA((23 + 6 * (N - 1),)),
        ],
        compiler_params=pltpu.CompilerParams(collective_id=0, has_side_effects=True),
    )(A.reshape(3, R, L), J.reshape(3, R, L), fixed.reshape(R, L), spin, offs.reshape(1, L),
      rel, eddy, loss, plane, axial, cap, prior, goal)
    misfit, dual, temp = pl.pallas_call(
        store,
        out_shape=tuple(jax.ShapeDtypeStruct(x.shape, f32) for x in (misfit, dual, temp)),
        in_specs=[vmem] * 3,
        out_specs=(hbm, hbm, hbm),
        scratch_shapes=[pltpu.SemaphoreType.DMA((3,))],
    )(*(pltpu.with_memory_space_constraint(x, pltpu.VMEM) for x in (misfit, dual, temp)))
    return misfit.reshape(3, 1, R, L), dual.reshape(3, 1, R, L), temp.reshape(1, R, L)


def solution(mesh):
    sizes = (mesh.shape["section"], mesh.shape["azim"], mesh.shape["axial"])
    in_specs = (
        P(None, "azim", "section", "axial"),
        P(None, "azim", "section", "axial"),
        P("azim", "section", "axial"),
        P(),
        P("axial"),
        P(),
        P(),
        P(),
        P(),
        P(),
        P(),
        P(None, ("section", "azim"), "axial"),
        P(None, ("section", "azim"), "axial"),
    )
    out_specs = (
        P(None, "azim", "section", "axial"),
        P(None, "azim", "section", "axial"),
        P("azim", "section", "axial"),
    )
    return jax.shard_map(functools.partial(body, sizes), mesh=mesh, in_specs=in_specs,
                         out_specs=out_specs, check_vma=False)
```

```python
import functools

import jax
import jax.numpy as jnp
from jax import lax
from jax.experimental import pallas as pl
from jax.experimental.pallas import tpu as pltpu
from jax.sharding import PartitionSpec as P

SWEEPS = 4
RIM = 8
MESH = pl.DeviceIdType.MESH


def pick(bits, table):
    low, mid, high = bits
    pairs = [jnp.where(low, table[2 * i + 1], table[2 * i]) for i in range(4)]
    return jnp.where(high, jnp.where(mid, pairs[3], pairs[2]), jnp.where(mid, pairs[1], pairs[0]))


def bits_of(regions):
    return ((regions & 1) != 0, (regions & 2) != 0, (regions & 4) != 0)


def kernel(sizes, *refs):
    S, N, C = sizes
    (A_hbm, J_hbm, fixed_hbm, spin_hbm, offs_hbm, *tables_hbm, prior, goal,
     misfit, dual, temp,
     turned, fixed, spin, offs, t_rel, t_eddy, t_loss, t_plane, t_axial, t_cap,
     AN, AX, AR, HN, HX, HR, regE, lossM, srcE, flux, H,
     priorX, goalX, regX, srcX, priorS, goalS, regS, srcS, priorP, goalP, regP, srcP,
     wa, wr, wl, inv, capH, rhsT, vT, vA, finT, finA, retA,
     A, J, edge, beside, relay, local, send, recv) = refs
    R, L = fixed.shape
    rows = prior.shape[1]
    RROT = spin.shape[1]
    ext = rows + 2 * RIM
    s, j, c = lax.axis_index("section"), lax.axis_index("azim"), lax.axis_index("axial")
    Q = S * N
    q = s * N + j

    def section_id(d):
        return (lax.rem(s + d + S, S), j, c)

    def axial_id(d):
        return (s, j, lax.rem(c + d + C, C))

    def azim_id(d):
        return (s, lax.rem(j + d + N, N), c)

    barrier = pltpu.get_barrier_semaphore()
    partners = [azim_id(d) for d in range(1, N)]
    partners += [near(d) for near in (section_id, axial_id) for d in (1, -1)]
    for partner in partners:
        pl.semaphore_signal(barrier, inc=1, device_id=partner, device_id_type=MESH)

    loads = [
        pltpu.make_async_copy(A_hbm, A, local.at[0]),
        pltpu.make_async_copy(goal, goalX.at[:, pl.ds(RIM, rows), :], local.at[1]),
        pltpu.make_async_copy(prior, priorX.at[:, pl.ds(RIM, rows), :], local.at[2]),
        pltpu.make_async_copy(J_hbm, J, local.at[3]),
    ]
    tables = (t_rel, t_eddy, t_loss, t_plane, t_axial, t_cap)
    maps = [pltpu.make_async_copy(src, dst, local.at[4 + k]) for k, (src, dst) in enumerate(
        zip((fixed_hbm, spin_hbm, offs_hbm, *tables_hbm), (fixed, spin, offs, *tables)))]
    loads = maps + loads
    for load in loads:
        load.start()
    loads = loads[len(maps):]

    used = [0, 0]
    pending = []
    finals = []

    def slots(sends=1, receives=1):
        first = tuple(used)
        used[0] += sends
        used[1] += receives
        return first

    def remote(src, dst, device, slot, d=0):
        return pltpu.make_async_remote_copy(
            src_ref=src, dst_ref=dst, send_sem=send.at[slot[0] + d], recv_sem=recv.at[slot[1] + d],
            device_id=device, device_id_type=MESH)

    def when(cond, f):
        if cond is None:
            f()
        else:
            pl.when(cond)(f)

    def unless(cond, f):
        when(None if cond is None else jnp.logical_not(cond), f)

    def copy(src, dst, device, sending=None, receiving=None, slot=None):
        desc = remote(src, dst, device, slot or slots())
        when(sending, lambda: desc.start())
        pending.append((desc, sending))
        return lambda: when(receiving, lambda: desc.wait_recv())

    def farthest(i):
        return jnp.where(j < N // 2, N - i, i)

    def both(*conds):
        return functools.reduce(jnp.logical_and, conds)

    top, bottom = j == 0, j == N - 1
    before, after = s > 0, s < S - 1

    up = lambda x, axis: pltpu.roll(x, x.shape[axis] - 1, axis)
    down = lambda x, axis: pltpu.roll(x, 1, axis)

    def each(f):
        if N <= 8:
            for a in range(N):
                f(a, (a + 1) % N, (a + N - 1) % N)
        else:
            def step(a, carry):
                f(a, lax.rem(a + 1, N), lax.rem(a + N - 1, N))
                return carry
            lax.fori_loop(0, N, step, 0)

    G = L // N
    assert G >= SWEEPS
    place = lax.broadcasted_iota(jnp.int32, (ext, L), 1) // G

    def forward(X, sides, packed):
        def add(a, ap, am):
            x = pltpu.roll(X[a], a * G, 1)
            first = isinstance(a, int) and a == 0
            packed[0] = x if first else jnp.where(place == a, x, packed[0])
            packed[1] = x if first else jnp.where(place == am, x, packed[1])
        each(add)
        return [copy(packed.at[0], sides.at[1], axial_id(-1), c > 0, c < C - 1),
                copy(packed.at[1], sides.at[0], axial_id(1), c < C - 1, c > 0)]

    def wide(X, sides, a):
        beside = jnp.where(place == a, sides[1], sides[0])
        return jnp.concatenate([X[a], pltpu.roll(beside, (L - a * G) % L, 1)], axis=1)

    half = RIM // 2
    assert half >= SWEEPS

    def rims(edge, beside, relay):
        upper = lax.broadcasted_iota(jnp.int32, (RIM, L), 0) < half

        def cut(a, ap, am):
            def tile(X, first):
                return X[a, first:first + RIM, :]
            edge[0, a] = jnp.where(upper, pltpu.roll(tile(priorX, rows), half, 0), tile(goalX, rows))
            edge[1, a] = jnp.where(upper, tile(goalX, RIM), pltpu.roll(tile(priorX, RIM), half, 0))
        each(cut)
        low, high, last, first = beside.at[0], beside.at[1], edge.at[0], edge.at[1]
        (to_next, at_low), (to_last, at_high), (turn_low, at_first), (turn_high, at_second) = (
            slots() for _ in range(4))
        arrivals = [
            copy(last, low, azim_id(1), jnp.logical_not(bottom), jnp.logical_not(top), (to_next, at_low)),
            copy(first, high, azim_id(-1), jnp.logical_not(top), jnp.logical_not(bottom), (to_last, at_high))]
        down_hop = copy(last, relay.at[0], azim_id(1), both(bottom, after), both(top, after),
                        (to_next, at_first))
        up_hop = copy(first, relay.at[1], section_id(-1), both(top, before), both(top, after),
                      (to_last, at_second))

        def early():
            up_hop()
            arrivals.append(copy(relay.at[1], high, azim_id(-1), both(top, after), both(bottom, after),
                                 (turn_high, at_high)))

        def late():
            down_hop()
            arrivals.append(copy(relay.at[0], low, section_id(1), both(top, after), both(top, before),
                                 (turn_low, at_low)))

            def arrived():
                for arrive in arrivals:
                    arrive()

                def spread_rims(a, ap, am):
                    for k, first in ((0, 0), (1, RIM + rows)):
                        goalX[a, first:first + RIM, :] = beside[k, a]
                        priorX[a, first:first + RIM, :] = pltpu.roll(beside[k, a], half, 0)
                each(spread_rims)
            return arrived
        return early, late

    def spread(E, target, known=lambda peer: None):
        inner = ext - RIM

        def block(peer, d, low, high, owner=j):
            first, count = (RIM if low else 0), (inner if low or high else ext)
            return remote(
                E.at[pl.ds(pl.multiple_of(peer * rows + first, 8), count), :],
                target.at[owner, pl.ds(first, count), :], (s, peer, c), k, d - 1)

        def cases(peer, f):
            pl.when(peer == 0)(lambda: f(True, False))
            pl.when(peer == N - 1)(lambda: f(False, True))
            pl.when(both(peer > 0, peer < N - 1))(lambda: f(False, False))

        k = slots(N - 1, N - 1)
        for i in range(1, N):
            d = farthest(i)
            peer = lax.rem(j + d, N)
            unless(known(peer), lambda: cases(
                peer, lambda low, high: block(peer, d, low, high).start()))
        for d in range(1, N):
            peer = lax.rem(j + d, N)
            finals.append(lambda peer=peer, d=d: unless(known(peer), lambda: cases(
                peer, lambda low, high: block(peer, d, low, high).wait_send())))
        edges = [copy(E.at[R:R + RIM, :], E.at[0:RIM, :], section_id(1), after, before),
                 copy(E.at[RIM:2 * RIM, :], E.at[R + RIM:R + 2 * RIM, :], section_id(-1), before, after)]

        def rest():
            for arrive in edges:
                arrive()
            ends = []
            _, come = slots(0, N - 1)
            for peer, start, there in ((0, 0, before), (N - 1, RIM + rows, after)):
                go, _ = slots(1, 0)
                d = lax.rem(peer - j + N, N)
                own = E.at[start if peer == 0 else R + RIM:(start if peer == 0 else R + RIM) + RIM, :]
                away = both(there, j != peer)
                desc = remote(own, target.at[j, pl.ds(start, RIM), :], (s, peer, c),
                              (go, come + jnp.where(d > 0, d - 1, 0)))
                pl.when(away)(lambda desc=desc: desc.start())
                pending.append((desc, away))
                for d in range(1, N):
                    got = remote(own, target.at[lax.rem(j - d + N, N), pl.ds(start, RIM), :],
                                 (s, peer, c), (go, come + d - 1))
                    ends.append((got, both(there, j == peer)))
            target[j] = E[pl.ds(pl.multiple_of(j * rows, 8), ext), :]

            def arrived():
                for d in range(1, N):
                    owner = lax.rem(j - d + N, N)
                    unless(known(j), lambda: cases(
                        j, lambda low, high: block(j, d, low, high, owner).wait_recv()))
                for got, here in ends:
                    pl.when(here)(lambda got=got: got.wait_recv())
            return arrived
        return rest

    pl.semaphore_wait(barrier, len(partners))

    got_an = copy(A_hbm.at[1:3], AN, azim_id(-1))
    got_ax = copy(A_hbm.at[0:2], AX, axial_id(-1), c > 0, c < C - 1)
    got_ar = copy(A_hbm.at[:, 0:RIM, :], AR, section_id(-1), before, after)

    for load in maps:
        load.wait()

    lane = lax.broadcasted_iota(jnp.int32, (R, L), 1)
    row = lax.broadcasted_iota(jnp.int32, (R, L), 0)
    for m in range(N):
        column = jnp.transpose(jnp.broadcast_to(spin[m:m + 1, :].astype(jnp.float32), (L, RROT)))
        turned[m, RIM:RIM + RROT, :] = column.astype(jnp.int32)

    def rotor(a, part, count):
        shift = a - offs[...]
        shift = jnp.broadcast_to(jnp.where(shift < 0, shift + N, shift), (count, L))
        value = turned[0, part, :]
        for m in range(1, N):
            value = jnp.where(shift == m, turned[m, part, :], value)
        return value

    def in_rotor(peer):
        return both(s == 0, (peer + 1) * rows + RIM <= RROT)

    regE[RIM:RIM + R, :] = fixed[...]
    regE[RIM:RIM + RROT, :] = jnp.where(s == 0, rotor(j, pl.ds(RIM, RROT), RROT), fixed[0:RROT, :])

    rest_reg = spread(regE, regX, in_rotor)
    loads[1].wait()
    loads[2].wait()
    rims_early, rims_late = rims(edge, beside, relay)
    lossM[...] = pick(bits_of(regE[RIM:RIM + R, :]), t_loss)
    got_reg = rest_reg()
    rims_early()

    loads[0].wait()

    got_ax()
    got_ar()
    last_lane, last_row = c == C - 1, s == S - 1

    def lane_up(values, beside):
        beside = jnp.where(last_lane, 0.0, beside)
        return pltpu.roll(jnp.where(lane == 0, beside, values), L - 1, 1)

    def row_up(values, beside):
        beside = jnp.where(last_row, 0.0, beside)
        return jnp.where(row == R - 1, beside, pltpu.roll(values, R - 1, 0))

    flux[0] = (row_up(A[2], AR[2, 0:1, :]) - A[2]) - (lane_up(A[1], AX[1]) - A[1])
    flux[1] = lane_up(A[0], AX[0]) - A[0]
    flux[2] = A[0] - row_up(A[0], AR[0, 0:1, :])
    got_an()
    f0 = flux[0]
    f1 = flux[1] - (AN[1] - A[2])
    f2 = flux[2] + (AN[0] - A[1])
    flux[1] = f1
    flux[2] = f2
    srcE[RIM:RIM + R, :] = lossM[...] * (f0 * f0 + f1 * f1 + f2 * f2)
    rest_src = spread(srcE, srcX)
    reluct = pick(bits_of(regE[RIM:RIM + R, :]), t_rel)
    H[0] = reluct * flux[0]
    H[1] = reluct * flux[1]
    H[2] = reluct * flux[2]
    got_hr = copy(H.at[:, R - RIM:R, :], HR, section_id(1), after, before)
    got_src = rest_src()
    ring = [remote(H.at[1 + i // 1], HN.at[i // 1], azim_id(1), slots()) for i in range(2)]
    pending.extend((piece, None) for piece in ring)
    pl.when(both(j == N - 1, s == 0))(lambda: ring[0].start())
    pl.when(both(j == N - 1, s == 0))(lambda: ring[1].start())

    got_rims = rims_late()

    got_reg()

    def own_rotor():
        def one(a, ap, am):
            regX[a] = rotor(a, pl.ds(pl.multiple_of(j * rows, 8), ext), ext)
        each(one)

    if RIM + rows <= RROT:
        pl.when(in_rotor(j))(own_rotor)
    got_reg = forward(regX, regS, regP)
    got_rims()
    pl.when(both(j == N - 1, s > 0, c % 2 == 0))(lambda: ring[0].start())
    pl.when(both(j < N - 1, c % 2 == 0))(lambda: ring[0].start())
    pl.when(both(j < N - 1, c % 2 == 0))(lambda: ring[1].start())
    got_goal = forward(goalX, goalS, goalP)
    got_prior = forward(priorX, priorS, priorP)

    got_src()
    got_src = forward(srcX, srcS, srcP)
    pl.when(both(j == N - 1, s > 0, c % 2 == 1))(lambda: ring[0].start())
    pl.when(both(j < N - 1, c % 2 == 1))(lambda: ring[0].start())
    pl.when(both(j < N - 1, c % 2 == 1))(lambda: ring[1].start())
    got_hx = copy(H.at[0:2], HX, axial_id(1), c < C - 1, c > 0)

    def ext_mask():
        grow = lax.broadcasted_iota(jnp.int32, (ext, 2 * L), 0) + (q * rows - RIM)
        glane = lax.broadcasted_iota(jnp.int32, (ext, 2 * L), 1)
        ok = jnp.logical_and(grow >= 0, grow < Q * rows)
        right = jnp.logical_and(glane >= L, glane < L + L // 2)
        left = glane >= L + L // 2
        ok = jnp.logical_and(ok, jnp.logical_not(jnp.logical_and(right, c == C - 1)))
        return jnp.logical_and(ok, jnp.logical_not(jnp.logical_and(left, c == 0)))

    for arrive in got_reg:
        arrive()

    def first(a, ap, am):
        bits = bits_of(wide(regX, regS, a))
        ok = ext_mask()
        plane = jnp.where(ok, pick(bits, t_plane), 0.0)
        axial = jnp.where(ok, pick(bits, t_axial), 0.0)
        capH[a] = pick(bits, t_cap)
        inv[a] = plane
        wr[a] = 0.5 * (plane + up(plane, 0))
        wl[a] = 0.5 * (axial + up(axial, 1))

    def second(a, ap, am):
        wa[a] = 0.5 * (inv[a] + inv[ap])

    def third(a, ap, am):
        total = (wa[a] + wa[am]) + (wr[a] + down(wr[a], 0)) + (wl[a] + down(wl[a], 1)) + capH[a]
        inv[a] = jnp.where(ext_mask(), 1.0 / total, 0.0)

    each(first)
    each(second)
    each(third)

    def inflow(v, a, ap, am):
        x = v[a]
        r, l = wr[a], wl[a]
        return ((wa[a] * v[ap] + wa[am] * v[am]) + (r * up(x, 0) + down(r * x, 0))
                + (l * up(x, 1) + down(l * x, 1)))

    for arrive in got_goal:
        arrive()

    def adjoint_first(a, ap, am):
        rhs = jnp.where(ext_mask(), wide(goalX, goalS, a), 0.0)
        rhsT[a] = rhs
        vA[0, a] = rhs * inv[a]

    each(adjoint_first)

    def sweeps(v, count, final):
        for k in range(count):
            now, later = k % 2, (k + 1) % 2

            def one(a, ap, am):
                new = (rhsT[a] + inflow(v.at[now], a, ap, am)) * inv[a]
                if k == count - 1:
                    final[a] = new[RIM:RIM + rows, 0:L]
                else:
                    v[later, a] = new
            each(one)

    def gather(final, ret):
        k = slots(N - 1, N - 1)

        def part(peer, d, owner=j):
            return remote(final.at[peer], ret.at[pl.ds(pl.multiple_of(owner * rows, 8), rows), :],
                          (s, peer, c), k, d - 1)

        for i in range(1, N):
            d = farthest(i)
            peer = lax.rem(j + d, N)
            part(peer, d).start()
        ret[pl.ds(pl.multiple_of(j * rows, 8), rows), :] = final[j]
        arrivals = []
        for d in range(1, N):
            pending.append((part(lax.rem(j + d, N), d), None))
            owner = lax.rem(j - d + N, N)
            arrivals.append(lambda d=d, owner=owner: part(j, d, owner).wait_recv())
        return arrivals

    sweeps(vA, SWEEPS - 1, finA)
    got_adj = gather(finA, retA)
    pl.when(both(j == N - 1, s > 0))(lambda: ring[1].start())

    for arrive in got_prior:
        arrive()
    for arrive in got_src:
        arrive()

    def thermal_first(a, ap, am):
        ok = ext_mask()
        start = jnp.where(ok, wide(priorX, priorS, a), 0.0)
        vT[0, a] = start
        rhsT[a] = capH[a] * start + jnp.where(ok, wide(srcX, srcS, a), 0.0)

    each(thermal_first)
    sweeps(vT, SWEEPS, finT)
    got_temp = gather(finT, temp)

    loads[3].wait()
    for piece in ring:
        piece.wait_recv()
    got_hx()
    got_hr()

    def lane_down(values, beside):
        beside = jnp.where(c == 0, 0.0, beside)
        return pltpu.roll(jnp.where(lane == L - 1, beside, values), 1, 1)

    def row_down(values, beside):
        beside = jnp.where(s == 0, 0.0, beside)
        return jnp.where(row == 0, beside, pltpu.roll(values, 1, 0))

    eddy = pick(bits_of(regE[RIM:RIM + R, :]), t_eddy)
    h0, h1, h2 = H[0], H[1], H[2]
    rim0, rim2 = HR[0, RIM - 1:RIM, :], HR[2, RIM - 1:RIM, :]
    misfit[0] = (lane_down(h1, HX[1]) - h1) - (row_down(h2, rim2) - h2) + eddy * A[0] - J[0]
    misfit[1] = (HN[1] - h2) - (lane_down(h0, HX[0]) - h0) + eddy * A[1] - J[1]
    misfit[2] = (row_down(h0, rim0) - h0) - (HN[0] - h1) + eddy * A[2] - J[2]

    for arrive in got_adj:
        arrive()
    scale = 2.0 * lossM[...] * retA[...]
    for k in range(3):
        dual[k] = scale * flux[k]
    for arrive in got_temp:
        arrive()
    for desc, sending in pending:
        when(sending, lambda: desc.wait_send())
    for final in finals:
        final()
    assert used == [send.shape[0], recv.shape[0]]


def store(*refs):
    sems = refs[6]
    copies = [pltpu.make_async_copy(refs[k], refs[3 + k], sems.at[k]) for k in range(3)]
    for one in copies:
        one.start()
    for one in copies:
        one.wait()


def body(sizes, *args):
    (A, J, fixed, spin, offs, rel, eddy, loss, plane, axial, cap, prior, goal) = args
    _, one, R, L = A.shape
    assert one == 1 and spin.shape[1] <= R
    S, N, C = sizes
    rows = prior.shape[1]
    ext = rows + 2 * RIM
    f32 = jnp.float32
    vmem = pl.BlockSpec(memory_space=pltpu.VMEM)
    hbm = pl.BlockSpec(memory_space=pl.ANY)
    V = lambda *shape, dtype=f32: pltpu.VMEM(shape, dtype)
    wide = (N, ext, 2 * L)
    misfit, dual, temp = pl.pallas_call(
        functools.partial(kernel, sizes),
        out_shape=(V(3, R, L), V(3, R, L), V(R, L)),
        in_specs=[hbm] * 13,
        out_specs=(vmem, vmem, vmem),
        scratch_shapes=[
            V(spin.shape[0], max(RIM + spin.shape[1], ext), L, dtype=jnp.int32),
            V(R, L, dtype=jnp.int32), V(*spin.shape, dtype=jnp.int32), V(1, L, dtype=jnp.int32),
            *[pltpu.SMEM(table.shape, f32) for table in (rel, eddy, loss, plane, axial, cap)],
            V(2, R, L), V(2, R, L), V(3, RIM, L), V(2, R, L), V(2, R, L), V(3, RIM, L),
            V(R + 2 * RIM, L, dtype=jnp.int32), V(R, L), V(R + 2 * RIM, L), V(3, R, L), V(3, R, L),
            V(N, ext, L), V(N, ext, L), V(N, ext, L, dtype=jnp.int32), V(N, ext, L),
            *[V(2, ext, L, dtype=kind) for kind in (f32, f32, jnp.int32, f32)] * 2,
            V(*wide), V(*wide), V(*wide), V(*wide), V(*wide), V(*wide), V(2, *wide), V(2, *wide),
            V(N, rows, L), V(N, rows, L), V(R, L), V(3, R, L), V(3, R, L),
            V(2, N, RIM, L), V(2, N, RIM, L), V(2, N, RIM, L), pltpu.SemaphoreType.DMA((13,)),
            pltpu.SemaphoreType.DMA((27 + 4 * (N - 1),)), pltpu.SemaphoreType.DMA((23 + 6 * (N - 1),)),
        ],
        compiler_params=pltpu.CompilerParams(collective_id=0, has_side_effects=True),
    )(A.reshape(3, R, L), J.reshape(3, R, L), fixed.reshape(R, L), spin, offs.reshape(1, L),
      rel, eddy, loss, plane, axial, cap, prior, goal)
    misfit, dual, temp = pl.pallas_call(
        store,
        out_shape=tuple(jax.ShapeDtypeStruct(x.shape, f32) for x in (misfit, dual, temp)),
        in_specs=[vmem] * 3,
        out_specs=(hbm, hbm, hbm),
        scratch_shapes=[pltpu.SemaphoreType.DMA((3,))],
    )(*(pltpu.with_memory_space_constraint(x, pltpu.VMEM) for x in (misfit, dual, temp)))
    return misfit.reshape(3, 1, R, L), dual.reshape(3, 1, R, L), temp.reshape(1, R, L)


def solution(mesh):
    sizes = (mesh.shape["section"], mesh.shape["azim"], mesh.shape["axial"])
    in_specs = (
        P(None, "azim", "section", "axial"),
        P(None, "azim", "section", "axial"),
        P("azim", "section", "axial"),
        P(),
        P("axial"),
        P(),
        P(),
        P(),
        P(),
        P(),
        P(),
        P(None, ("section", "azim"), "axial"),
        P(None, ("section", "azim"), "axial"),
    )
    out_specs = (
        P(None, "azim", "section", "axial"),
        P(None, "azim", "section", "axial"),
        P("azim", "section", "axial"),
    )
    return jax.shard_map(functools.partial(body, sizes), mesh=mesh, in_specs=in_specs,
                         out_specs=out_specs, check_vma=False)
```
